32 devices in a mesh: groups: 2 (over y), row: 16 (over z, x, core).
Axes of the slice: x: 2, y: 2, z: 4, core: 2. Of those that a mesh axis runs over, the one named last changes fastest.
Arguments:
- layer_input: bfloat16 [8192, 512], P('row', 'groups'), parts along dimension 1, may hold values from -6 to 6
- output_grad: bfloat16 [8192, 512], P('row', 'groups'), parts along dimension 1, may hold values from -1.5 to 1.5
- gate_weight: bfloat16 [28672, 8192], P(('groups', 'row')), parts along dimension 0, may hold values from -0.09375 to 0.09375
- up_weight: bfloat16 [28672, 8192], P(('groups', 'row')), parts along dimension 0, may hold values from -0.09375 to 0.09375
- down_weight: bfloat16 [28672, 8192], P(('groups', 'row')), parts along dimension 0, may hold values from -0.046875 to 0.046875
Outputs:
- input_grad: bfloat16 [8192, 512], P('row', 'groups'), parts along dimension 1
- gate_grad: bfloat16 [28672, 8192], P(('groups', 'row')), parts along dimension 0
- up_grad: bfloat16 [28672, 8192], P(('groups', 'row')), parts along dimension 0
- down_grad: bfloat16 [28672, 8192], P(('groups', 'row')), parts along dimension 0
The draws below stay inside these ranges and needn't reach their ends.
There are 2 independent parts, one for each index of `groups`. The reference program is written for one: setup_inputs(seed, part) draws one part's arguments, and reference() takes and returns one part's arrays. A program takes and returns all parts, laid end to end along the dimension named above; each array names one. Nothing has to cross between parts.
All inputs are finite; a program needn't handle non-finite values.
Results may differ from the reference program's by a relative error of at most 0.0049.
Values may be sent and summed in bfloat16 or wider, within the bound.
A program may use at most 192 MiB of HBM per device.

```python
import jax
import jax.numpy as jnp

D = 8192
FF = 14336
TOKENS = 256


def raised(drawn, own_key, source, target, blocks, factor):
    def block_of(position):
        return (jnp.arange(drawn.shape[position]) // (drawn.shape[position] // blocks)).reshape((-1,) + (1,) * (drawn.ndim - 1 - position))

    one_side = jax.random.permutation(own_key, blocks)[block_of(target)]
    far = (block_of(target) + blocks // 2) % blocks
    return jnp.where((block_of(source) == one_side) | (block_of(source) == far), factor * drawn, drawn)


def block_scale(stream_key, shape, cuts, least, top_value):
    def one(dim, shards_of):
        steps = jax.random.uniform(jax.random.fold_in(jax.random.fold_in(stream_key, 6), dim), (shards_of,), jnp.float32, least / len(cuts), top_value / len(cuts))
        return jnp.repeat(jnp.exp(steps), shape[dim] // shards_of).reshape((-1,) + (1,) * (len(shape) - dim - 1))

    factor_of = one(*cuts[0])
    for cut in cuts[1:]:
        factor_of = factor_of * one(*cut)
    return factor_of


def noise(stream_key, extent, width, limit, split=(), kind=jnp.bfloat16):
    loudness = block_scale(stream_key, extent, split, -0.22, 0.18) if split else 1.0
    entries = jax.random.normal(stream_key, extent, jnp.float32) * width * loudness
    return jnp.minimum(jnp.maximum(entries, -limit), limit).astype(kind)


def heavy_noise(key, extent, scale, reach, shards, heavy, dtype=jnp.bfloat16):
    result = scale * jax.random.normal(key, extent, jnp.float32)
    if shards:
        result = result * block_scale(key, extent, shards, -0.22, 0.18)
    return jnp.clip(raised(result, jax.random.fold_in(key, 3), *heavy), -reach, reach).astype(dtype)


def setup_inputs(seed: int = 0, part: int = 0) -> dict:
    keys = jax.random.split(jax.random.key(seed), 6)
    own_keys = jax.random.split(jax.random.fold_in(keys[5], part), 6)
    layer_input = noise(own_keys[0], (D, TOKENS), 1.0, 6.0, ((0, 16),))
    output_grad = noise(own_keys[1], (D, TOKENS), 0.25, 1.5, ((0, 16),))
    gate_weight = heavy_noise(own_keys[2], (FF, D), D ** -0.5, 0.09375, ((0, 16),), (0, 1, 16, 2.0))
    up_weight = heavy_noise(own_keys[3], (FF, D), D ** -0.5, 0.09375, ((0, 16),), (0, 1, 16, 2.0))
    down_weight = noise(own_keys[4], (FF, D), FF ** -0.5, 0.046875, ((0, 16),))
    return dict(layer_input=layer_input, output_grad=output_grad, gate_weight=gate_weight, up_weight=up_weight, down_weight=down_weight)


def reference(layer_input, output_grad, gate_weight, up_weight, down_weight):
    gate_pre = jnp.dot(gate_weight, layer_input, preferred_element_type=jnp.float32)
    up_pre = jnp.dot(up_weight, layer_input, preferred_element_type=jnp.float32)
    sig = jax.nn.sigmoid(gate_pre)
    act = gate_pre * sig
    hidden_act = (act * up_pre).astype(jnp.bfloat16)
    hidden_grad = jnp.dot(down_weight, output_grad, preferred_element_type=jnp.float32)
    grad_gate_pre = (hidden_grad * up_pre * sig * (1.0 + gate_pre * (1.0 - sig))).astype(jnp.bfloat16)
    grad_up_pre = (hidden_grad * act).astype(jnp.bfloat16)
    down_grad = jnp.dot(hidden_act, output_grad.T, preferred_element_type=jnp.float32).astype(jnp.bfloat16)
    gate_grad = jnp.dot(grad_gate_pre, layer_input.T, preferred_element_type=jnp.float32).astype(jnp.bfloat16)
    up_grad = jnp.dot(grad_up_pre, layer_input.T, preferred_element_type=jnp.float32).astype(jnp.bfloat16)
    input_grad = jnp.dot(gate_weight.T, grad_gate_pre, preferred_element_type=jnp.float32)
    input_grad = input_grad + jnp.dot(up_weight.T, grad_up_pre, preferred_element_type=jnp.float32)
    return input_grad.astype(jnp.bfloat16), gate_grad, up_grad, down_grad
```

```python
import functools

import jax
import jax.numpy as jnp
from jax import lax
from jax.experimental import pallas as pl
from jax.experimental.pallas import tpu as pltpu
from jax.sharding import PartitionSpec as P

MESH = pl.DeviceIdType.MESH
VMEM_LIMIT = 64 * 1000 * 1000
GRID_VMEM = 64 * 1024 * 1024


def over_tokens(first_mat, second_mat):
    return lax.dot_general(
        first_mat, second_mat, (((1,), (1,)), ((), ())), preferred_element_type=jnp.float32
    )


def nearest(rank, here, extent):
    low = jnp.minimum(here, extent - 1 - here)
    half = (rank + 1) // 2
    both = jnp.where(rank % 2 == 1, here + half, here - half)
    one = jnp.where(here < extent - 1 - here, rank, extent - 1 - rank)
    return jnp.where(rank <= 2 * low, both, one)


def place(zs, xs):
    me = lax.axis_index("row")
    core = me % 2
    x = (me // 2) % xs
    z = me // (2 * xs)
    return z, x, core


def chip_at(step, z, x, zs, xs):
    if xs == 2:
        inner = (step > 0) & (step < 2 * zs - 1)
        beside = jnp.where(inner, (step + 1) % 2, jnp.minimum(step, 1))
        rank = jnp.where(inner, (step + 1) // 2 - beside, step // 2)
    else:
        rank, beside = step // xs, step % xs
    cz = nearest(rank, z, zs)
    cx = nearest(beside, x, xs)
    return cz, cx, cz * xs + cx


def greet(z, x, core, zs, xs):
    barrier = pltpu.get_barrier_semaphore()

    def hail(cz, cx, cc):
        pl.semaphore_signal(
            barrier, inc=1, device_id={"row": (cz * xs + cx) * 2 + cc}, device_id_type=MESH
        )

    hail(z, x, 1 - core)
    pl.when(z > 0)(lambda: hail(z - 1, x, core))
    pl.when(z < zs - 1)(lambda: hail(z + 1, x, core))
    pl.when(x > 0)(lambda: hail(z, x - 1, core))
    pl.when(x < xs - 1)(lambda: hail(z, x + 1, core))
    count = 1 + jnp.minimum(z, 1) + jnp.minimum(zs - 1 - z, 1)
    count = count + jnp.minimum(x, 1) + jnp.minimum(xs - 1 - x, 1)
    pl.semaphore_wait(barrier, count)


def forward_kernel(
    zs, xs, x_ref, dy_ref, wg_ref, wu_ref, wd_ref,
    hact_ref, ggp_ref, gup_ref, ggp_t_ref, gup_t_ref, xg_ref, dyg_ref,
    held, wbuf, acc, send_sem, recv_sem, wsem, own_sem, out_sem,
):
    z, x, core = place(zs, xs)
    mine = z * xs + x
    chips = zs * xs
    rows, hidden = held.shape[3], acc.shape[1]
    width = 2 * rows
    tokens = held.shape[4]

    def weights(step, fn):
        _, _, chip = chip_at(step, z, x, zs, xs)
        cols = pl.ds(pl.multiple_of(chip * width, 128), width)
        slot = step % 2
        for n, ref in enumerate((wg_ref, wu_ref, wd_ref)):
            fn(pltpu.make_async_copy(ref.at[:, cols], wbuf.at[slot, n], wsem.at[slot, n]))

    weights(0, lambda c: c.start())
    own = [
        pltpu.make_async_copy(ref, held.at[mine, n, core], own_sem.at[n])
        for n, ref in enumerate((x_ref, dy_ref))
    ]
    for c in own:
        c.start()
    greet(z, x, core, zs, xs)
    for c in own:
        c.wait()

    def passing(step, fn):
        cz, cx, chip = chip_at(step, z, x, zs, xs)
        block = held.at[chip, :, core]

        def copy(tz, tx, tc, n):
            return lambda: fn(
                pltpu.make_async_remote_copy(
                    src_ref=block,
                    dst_ref=block,
                    send_sem=send_sem.at[n, chip],
                    recv_sem=recv_sem.at[chip, core],
                    device_id={"row": (tz * xs + tx) * 2 + tc},
                    device_id_type=MESH,
                )
            )

        pl.when((cx == x) & (cz <= z) & (z < zs - 1))(copy(z + 1, x, core, 0))
        pl.when((cx == x) & (cz >= z) & (z > 0))(copy(z - 1, x, core, 1))
        pl.when((cx <= x) & (x < xs - 1))(copy(z, x + 1, core, 2))
        pl.when((cx >= x) & (x > 0))(copy(z, x - 1, core, 3))
        copy(z, x, 1 - core, 4)()

    def arrive(step, which):
        _, _, chip = chip_at(step, z, x, zs, xs)
        block = held.at[chip, :, which]
        pltpu.make_async_copy(block, block, recv_sem.at[chip, which]).wait()

    passing(0, lambda c: c.start())
    acc[...] = jnp.zeros_like(acc)

    def body(step, carry):
        @pl.when(step + 1 < chips)
        def _():
            weights(step + 1, lambda c: c.start())
            arrive(step + 1, core)
            passing(step + 1, lambda c: c.start())

        arrive(step, 1 - core)
        weights(step, lambda c: c.wait())
        _, _, chip = chip_at(step, z, x, zs, xs)
        for n, ref in enumerate((xg_ref, dyg_ref)):
            pltpu.make_async_copy(held.at[chip, n], ref.at[chip], out_sem.at[n, chip]).start()
        slot = step % 2
        x_block = held[chip, 0].reshape(width, tokens)
        acc[0] += jnp.dot(wbuf[slot, 0], x_block, preferred_element_type=jnp.float32)
        acc[1] += jnp.dot(wbuf[slot, 1], x_block, preferred_element_type=jnp.float32)
        dy_block = held[chip, 1].reshape(width, tokens)
        acc[2] += jnp.dot(wbuf[slot, 2], dy_block, preferred_element_type=jnp.float32)
        return carry

    lax.fori_loop(0, chips, body, 0)

    part = 128 if hidden % 128 == 0 else hidden
    for start in range(0, hidden, part):
        at = slice(start, start + part)
        gate_pre, up_pre, hidden_grad = acc[0, at], acc[1, at], acc[2, at]
        sig = jax.nn.sigmoid(gate_pre)
        act = gate_pre * sig
        hact_ref[at] = (act * up_pre).astype(jnp.bfloat16)
        grad_gate_pre = hidden_grad * up_pre * sig * (1.0 + gate_pre * (1.0 - sig))
        ggp_ref[at] = grad_gate_pre.astype(jnp.bfloat16)
        ggp_t_ref[:, at] = grad_gate_pre.T.astype(jnp.bfloat16)
        grad_up_pre = hidden_grad * act
        gup_ref[at] = grad_up_pre.astype(jnp.bfloat16)
        gup_t_ref[:, at] = grad_up_pre.T.astype(jnp.bfloat16)

    def drain(step, carry):
        _, _, chip = chip_at(step, z, x, zs, xs)
        passing(step, lambda c: c.wait_send())
        for n, ref in enumerate((xg_ref, dyg_ref)):
            pltpu.make_async_copy(held.at[chip, n], ref.at[chip], out_sem.at[n, chip]).wait()
        return carry

    lax.fori_loop(0, chips, drain, 0)


def scatter_kernel(
    zs, xs, ggp_ref, gup_ref, wg_ref, wu_ref, out_ref,
    wbuf, part, core_out, core_in, line_out, x_in, z_in,
    wsem, core_send, core_recv, line_send, x_recv, z_recv,
):
    z, x, core = place(zs, xs)
    chips = zs * xs
    rows, tokens = out_ref.shape
    width = 2 * rows

    def chip_of(step):
        return chip_at(chips - 1 - step, z, x, zs, xs)

    def weights(step, fn):
        _, _, chip = chip_of(step)
        cols = pl.ds(pl.multiple_of(chip * width, 128), width)
        slot = step % 2
        for n, ref in enumerate((wg_ref, wu_ref)):
            fn(pltpu.make_async_copy(ref.at[:, cols], wbuf.at[slot, n], wsem.at[slot, n]))

    def to_core(chip):
        return pltpu.make_async_remote_copy(
            src_ref=core_out.at[chip],
            dst_ref=core_in.at[chip],
            send_sem=core_send.at[chip],
            recv_sem=core_recv.at[chip],
            device_id={"row": (z * xs + x) * 2 + 1 - core},
            device_id_type=MESH,
        )

    def line(chip, tz, tx, buf, sems, side):
        return pltpu.make_async_remote_copy(
            src_ref=line_out.at[chip],
            dst_ref=buf.at[side, chip],
            send_sem=line_send.at[chip],
            recv_sem=sems.at[side, chip],
            device_id={"row": (tz * xs + tx) * 2 + core},
            device_id_type=MESH,
        )

    def onward(cz, cx, chip, fn):
        pl.when(cx > x)(lambda: fn(line(chip, z, x + 1, x_in, x_recv, 0)))
        pl.when(cx < x)(lambda: fn(line(chip, z, x - 1, x_in, x_recv, 1)))
        pl.when((cx == x) & (cz > z))(lambda: fn(line(chip, z + 1, x, z_in, z_recv, 0)))
        pl.when((cx == x) & (cz < z))(lambda: fn(line(chip, z - 1, x, z_in, z_recv, 1)))

    weights(0, lambda c: c.start())
    greet(z, x, core, zs, xs)

    def make(step):
        slot = step % 2
        _, _, chip = chip_of(step)

        @pl.when(step + 1 < chips)
        def _():
            weights(step + 1, lambda c: c.start())

        weights(step, lambda c: c.wait())
        total = jnp.dot(ggp_ref[...], wbuf[slot, 0], preferred_element_type=jnp.float32)
        total += jnp.dot(gup_ref[...], wbuf[slot, 1], preferred_element_type=jnp.float32)
        part[slot] = total.T.reshape(2, rows, tokens)
        core_out[chip] = part[slot, 1 - core].astype(jnp.bfloat16)
        to_core(chip).start()

    def add(step):
        slot = step % 2
        cz, cx, chip = chip_of(step)
        to_core(chip).wait_recv()
        part[slot, core] += core_in[chip].astype(jnp.float32)

        def take(buf, sems, side):
            def run():
                block = buf.at[side, chip]
                pltpu.make_async_copy(block, block, sems.at[side, chip]).wait()
                part[slot, core] += buf[side, chip].astype(jnp.float32)

            return run

        pl.when((cx >= x) & (x > 0))(take(x_in, x_recv, 0))
        pl.when((cx <= x) & (x < xs - 1))(take(x_in, x_recv, 1))
        pl.when((cx == x) & (cz >= z) & (z > 0))(take(z_in, z_recv, 0))
        pl.when((cx == x) & (cz <= z) & (z < zs - 1))(take(z_in, z_recv, 1))
        line_out[chip] = part[slot, core].astype(jnp.bfloat16)
        onward(cz, cx, chip, lambda c: c.start())

    make(0)

    def body(step, carry):
        make(step)
        add(step - 1)
        return carry

    lax.fori_loop(1, chips, body, 0)
    add(chips - 1)
    out_ref[...] = line_out[z * xs + x]

    def drain(step, carry):
        cz, cx, chip = chip_of(step)
        to_core(chip).wait_send()
        onward(cz, cx, chip, lambda c: c.wait_send())
        return carry

    lax.fori_loop(0, chips, drain, 0)


def on_device(zs, xs, layer_input, output_grad, gate_weight, up_weight, down_weight):
    chips = zs * xs
    rows, tokens = layer_input.shape
    hidden, features = gate_weight.shape
    width = 2 * rows
    bf16, f32 = jnp.bfloat16, jnp.float32
    anywhere = pl.BlockSpec(memory_space=pl.ANY)
    vmem = pl.BlockSpec(memory_space=pltpu.VMEM)
    DMA = pltpu.SemaphoreType.DMA
    small = jax.ShapeDtypeStruct((hidden, tokens), bf16)
    turned = jax.ShapeDtypeStruct((tokens, hidden), bf16)
    whole = jax.ShapeDtypeStruct((chips, 2, rows, tokens), bf16)
    hidden_act, ggp, gup, ggp_t, gup_t, xg, dyg = pl.pallas_call(
        functools.partial(forward_kernel, zs, xs),
        out_shape=(small, small, small, turned, turned, whole, whole),
        in_specs=[anywhere] * 5,
        out_specs=(vmem, vmem, vmem, vmem, vmem, anywhere, anywhere),
        scratch_shapes=[
            pltpu.VMEM((chips, 2, 2, rows, tokens), bf16),
            pltpu.VMEM((2, 3, hidden, width), bf16),
            pltpu.VMEM((3, hidden, tokens), f32),
            DMA((5, chips)),
            DMA((chips, 2)),
            DMA((2, 3)),
            DMA((2,)),
            DMA((2, chips)),
        ],
        compiler_params=pltpu.CompilerParams(
            collective_id=0, has_side_effects=True, vmem_limit_bytes=VMEM_LIMIT
        ),
        name="gather_forward",
    )(layer_input, output_grad, gate_weight, up_weight, down_weight)
    input_grad = pl.pallas_call(
        functools.partial(scatter_kernel, zs, xs),
        out_shape=jax.ShapeDtypeStruct((rows, tokens), bf16),
        in_specs=[vmem, vmem, anywhere, anywhere],
        out_specs=vmem,
        scratch_shapes=[
            pltpu.VMEM((2, 2, hidden, width), bf16),
            pltpu.VMEM((2, 2, rows, tokens), f32),
            pltpu.VMEM((chips, rows, tokens), bf16),
            pltpu.VMEM((chips, rows, tokens), bf16),
            pltpu.VMEM((chips, rows, tokens), bf16),
            pltpu.VMEM((2, chips, rows, tokens), bf16),
            pltpu.VMEM((2, chips, rows, tokens), bf16),
            DMA((2, 2)),
            DMA((chips,)),
            DMA((chips,)),
            DMA((chips,)),
            DMA((2, chips)),
            DMA((2, chips)),
        ],
        compiler_params=pltpu.CompilerParams(
            collective_id=1, has_side_effects=True, vmem_limit_bytes=VMEM_LIMIT
        ),
        name="scatter_input_grad",
    )(ggp_t, gup_t, gate_weight, up_weight)
    block_in = xg.reshape(features, tokens)
    block_dy = dyg.reshape(features, tokens)
    down_grad = over_tokens(hidden_act, block_dy).astype(bf16)
    gate_grad = over_tokens(ggp, block_in).astype(bf16)
    up_grad = over_tokens(gup, block_in).astype(bf16)
    return (input_grad, gate_grad, up_grad, down_grad)


EVENTS = (
    (16, 17, 5, 4, 2, 18, 19, 20, 8, 3, 21, 22, 12, 7, 6, 23, 10, 9, 24, 25, 26, 13, 27, 14, 28, 29, 32, 15,
     11, 30, 31),
    (16, 17, 8, 0, 18, 19, 9, 20, 10, 6, 12, 7, 1, 21, 22, 23, 24, 2, 25, 26, 3, 13, 27, 28, 11, 29, 15, 14,
     30, 31, 32),
)
USE = (
    (0, 1, 5, 4, 2, 8, 3, 12, 6, 10, 7, 9, 13, 14, 15, 11),
    (4, 5, 8, 0, 9, 10, 6, 12, 7, 1, 2, 3, 13, 11, 15, 14),
)
GIVE = (
    (7, 6, 22, 23, 5, 21, 4, 18, 19, 0, 20, 3, 2, 16, 14, 15, 1, 17, 10, 12, 11, 13, 8, 9),
    (7, 1, 22, 6, 10, 2, 5, 4, 18, 19, 0, 3, 23, 14, 15, 21, 11, 20, 9, 16, 8, 17, 12, 13),
)


def listed(rows, inside):
    return [jnp.where(inside, b, a) for a, b in zip(*rows)]


def entry(values, step):
    found = values[0]
    for n, value in enumerate(values[1:], 1):
        found = jnp.where(step == n, value, found)
    return found


def grid_kernel(
    x_ref, dy_ref, wg_ref, wu_ref, wd_ref,
    grad_ref, hact_ref, ggp_ref, gup_ref, all_ref,
    held, wgu, wdn, acc, hact, ggp, gup, ggp_t, gup_t, part, outb, core_in, x_in, z_in,
    own_sem, wsem, send_sem, recv_sem, all_sem, small_sem,
    core_send, core_recv, line_send, x_recv, z_recv,
):
    zs, xs = 4, 2
    z, x, core = place(zs, xs)
    mine = z * xs + x
    rows, hidden, tokens = held.shape[3], acc.shape[1], acc.shape[2]
    width = 2 * rows
    half = rows // 2
    low = z < 2
    inside = (z > 0) & (z < 3)
    events = listed(EVENTS, inside)
    use = listed(USE, inside)
    give = listed(GIVE, inside)
    f32, bf16 = jnp.float32, jnp.bfloat16

    def target(cz, cx, cc):
        return {"row": (cz * xs + cx) * 2 + cc}

    def piece_at(code):
        near = code // 4
        cz = jnp.where(low, near, 3 - near)
        cx = jnp.where((code // 2) % 2 == 1, 1 - x, x)
        return cz, cx, cz * xs + cx, code % 2

    def weights(step, fn):
        _, _, chip, n = piece_at(entry(use, step))
        slot = step % 3
        cols = pl.ds(pl.multiple_of(chip * width, 128), width)

        @pl.when(n == 0)
        def _():
            fn(pltpu.make_async_copy(wg_ref.at[:, cols], wgu.at[chip, 0], wsem.at[slot, 0]))
            fn(pltpu.make_async_copy(wu_ref.at[:, cols], wgu.at[chip, 1], wsem.at[slot, 1]))

        @pl.when(n == 1)
        def _():
            fn(pltpu.make_async_copy(wd_ref.at[:, cols], wdn.at[slot], wsem.at[slot, 0]))

    def passing(cz, cx, chip, n, src, fn):
        two = ((cz == 0) | (cz == zs - 1)) & (n == 1)
        column = cx == x
        along = column | two

        def copy(tz, tx, tc, way):
            return lambda: fn(
                pltpu.make_async_remote_copy(
                    src_ref=src,
                    dst_ref=held.at[chip, n, core],
                    send_sem=send_sem.at[way, chip, n],
                    recv_sem=recv_sem.at[chip, n, core],
                    device_id=target(tz, tx, tc),
                    device_id_type=MESH,
                )
            )

        pl.when(along & (cz <= z) & (z < zs - 1))(copy(z + 1, x, core, 0))
        pl.when(along & (cz >= z) & (z > 0))(copy(z - 1, x, core, 1))
        pl.when(column & (jnp.logical_not(two) | (cz == z)))(copy(z, 1 - x, core, 2))
        copy(z, x, 1 - core, 3)()

    def arrive(chip, n, which):
        block = held.at[chip, n, which]
        pltpu.make_async_copy(block, block, recv_sem.at[chip, n, which]).wait()

    own = [
        pltpu.make_async_copy(ref, held.at[mine, n, core], own_sem.at[n])
        for n, ref in enumerate((x_ref, dy_ref))
    ]
    for c in own:
        c.start()
    greet(z, x, core, zs, xs)
    for n, ref in enumerate((x_ref, dy_ref)):
        passing(z, x, mine, n, ref, lambda c: c.start())
    weights(0, lambda c: c.start())
    weights(1, lambda c: c.start())
    acc[...] = jnp.zeros_like(acc)
    for c in own:
        c.wait()

    part_rows = 128 if hidden % 128 == 0 else hidden

    def gather(step, carry):
        event = entry(events, step)

        @pl.when(event < 16)
        def _():
            cz, cx, chip, n = piece_at(event)
            arrive(chip, n, core)
            passing(cz, cx, chip, n, held.at[chip, n, core], lambda c: c.start())

        @pl.when((event >= 16) & (event < 32))
        def _():
            count = event - 16
            cz, cx, chip, n = piece_at(entry(use, count))
            pl.when(count + 2 < 16)(lambda: weights(count + 2, lambda c: c.start()))
            arrive(chip, n, 1 - core)
            pltpu.make_async_copy(held.at[chip, n], all_ref.at[n, chip], all_sem.at[n, chip]).start()
            weights(count, lambda c: c.wait())

            @pl.when(n == 0)
            def _():
                block = held[chip, 0].reshape(width, tokens)
                acc[0] += jnp.dot(wgu[chip, 0], block, preferred_element_type=f32)
                acc[1] += jnp.dot(wgu[chip, 1], block, preferred_element_type=f32)

            @pl.when(n == 1)
            def _():
                block = held[chip, 1].reshape(width, tokens)
                acc[2] += jnp.dot(wdn[count % 3], block, preferred_element_type=f32)

        @pl.when(event == 32)
        def _():
            for start in range(0, hidden, part_rows):
                at = slice(start, start + part_rows)
                gate_pre, up_pre = acc[0, at], acc[1, at]
                sig = jax.nn.sigmoid(gate_pre)
                act = gate_pre * sig
                hact[at] = (act * up_pre).astype(bf16)
                acc[0, at] = up_pre * sig * (1.0 + gate_pre * (1.0 - sig))
                acc[1, at] = act

        return carry

    lax.fori_loop(0, len(EVENTS[0]), gather, 0)

    for start in range(0, hidden, part_rows):
        at = slice(start, start + part_rows)
        hidden_grad = acc[2, at]
        grad_gate_pre = (hidden_grad * acc[0, at]).astype(bf16)
        grad_up_pre = (hidden_grad * acc[1, at]).astype(bf16)
        ggp[at] = grad_gate_pre
        ggp_t[:, at] = grad_gate_pre.T
        gup[at] = grad_up_pre
        gup_t[:, at] = grad_up_pre.T
    small = [
        pltpu.make_async_copy(src, dst, small_sem.at[n])
        for n, (src, dst) in enumerate(((hact, hact_ref), (ggp, ggp_ref), (gup, gup_ref)))
    ]
    for c in small:
        c.start()

    def to_core(chip, h):
        at = pl.ds(pl.multiple_of(h * tokens, tokens), tokens)
        return pltpu.make_async_remote_copy(
            src_ref=outb.at[chip, at],
            dst_ref=core_in.at[chip, at],
            send_sem=core_send.at[chip, h],
            recv_sem=core_recv.at[chip, h],
            device_id=target(z, x, 1 - core),
            device_id_type=MESH,
        )

    def onward(cz, cx, chip, h, fn):
        two = ((cz == 0) | (cz == zs - 1)) & (h == 1)
        along = (cx == x) | two
        at = pl.ds(pl.multiple_of(h * tokens, tokens), tokens)

        def line(tz, tx, dst, sem):
            return lambda: fn(
                pltpu.make_async_remote_copy(
                    src_ref=outb.at[chip, at],
                    dst_ref=dst,
                    send_sem=line_send.at[chip, h],
                    recv_sem=sem,
                    device_id=target(tz, tx, core),
                    device_id_type=MESH,
                )
            )

        pl.when(along & (cz > z))(line(z + 1, x, z_in.at[0, chip, at], z_recv.at[0, chip, h]))
        pl.when(along & (cz < z))(line(z - 1, x, z_in.at[1, chip, at], z_recv.at[1, chip, h]))
        pl.when((cx != x) & (jnp.logical_not(two) | (cz == z)))(
            line(z, 1 - x, x_in.at[cz, at], x_recv.at[cz, h])
        )

    def block_at(code):
        near = code // 2
        cz = jnp.where(low, near, 3 - near)
        cx = jnp.where(code % 2 == 1, 1 - x, x)
        return cz, cx, cz * xs + cx

    def scatter(step, carry):
        code = entry(give, step)

        @pl.when(code < 8)
        def _():
            _, _, chip = block_at(code)

            def product(which):
                cols = pl.ds(pl.multiple_of(which * rows, 128), rows)
                total = jnp.dot(ggp_t[...], wgu[chip, 0, :, cols], preferred_element_type=f32)
                return total + jnp.dot(gup_t[...], wgu[chip, 1, :, cols], preferred_element_type=f32)

            total = product(1 - core)
            for h in range(2):
                at = slice(h * tokens, (h + 1) * tokens)
                outb[chip, at] = total[:, h * half : (h + 1) * half].astype(bf16)
                to_core(chip, h).start()
            total = product(core)
            for h in range(2):
                at = slice(h * tokens, (h + 1) * tokens)
                part[chip, at] = total[:, h * half : (h + 1) * half]

        @pl.when(code >= 8)
        def _():
            h = code % 2
            cz, cx, chip = block_at((code - 8) // 2)
            two = ((cz == 0) | (cz == zs - 1)) & (h == 1)
            along = (cx == x) | two
            at = pl.ds(pl.multiple_of(h * tokens, tokens), tokens)
            to_core(chip, h).wait()
            part[chip, at] += core_in[chip, at].astype(f32)

            def gain(block, sem):
                def run():
                    pltpu.make_async_copy(block, block, sem).wait()
                    part[chip, at] += block[...].astype(f32)

                return run

            pl.when((cx == x) & (jnp.logical_not(two) | (cz == z)))(
                gain(x_in.at[cz, at], x_recv.at[cz, h])
            )
            pl.when(along & (cz >= z) & (z > 0))(gain(z_in.at[0, chip, at], z_recv.at[0, chip, h]))
            pl.when(along & (cz <= z) & (z < zs - 1))(
                gain(z_in.at[1, chip, at], z_recv.at[1, chip, h])
            )
            outb[chip, at] = part[chip, at].astype(bf16)
            onward(cz, cx, chip, h, lambda c: c.start())

        return carry

    lax.fori_loop(0, len(GIVE[0]), scatter, 0)
    grad_ref[...] = outb[mine]

    for c in small:
        c.wait()

    def drain(step, carry):
        cz, cx, chip, n = piece_at(step)
        passing(cz, cx, chip, n, held.at[chip, n, core], lambda c: c.wait_send())
        pltpu.make_async_copy(held.at[chip, n], all_ref.at[n, chip], all_sem.at[n, chip]).wait()
        onward(cz, cx, chip, n, lambda c: c.wait_send())
        return carry

    lax.fori_loop(0, 16, drain, 0)


def weight_grads_kernel(
    hact_ref, ggp_ref, gup_ref, x_ref, dy_ref, turned_ref, gate_ref, up_ref, down_ref, grad_ref
):
    bf16 = jnp.bfloat16
    gate_ref[...] = over_tokens(ggp_ref[...], x_ref[0]).astype(bf16)
    up_ref[...] = over_tokens(gup_ref[...], x_ref[0]).astype(bf16)
    down_ref[...] = over_tokens(hact_ref[...], dy_ref[0]).astype(bf16)

    @pl.when(pl.program_id(0) == 0)
    def _():
        tokens = grad_ref.shape[1]
        half = grad_ref.shape[0] // 2
        for h in range(2):
            grad_ref[h * half : (h + 1) * half] = turned_ref[h * tokens : (h + 1) * tokens].T


def on_grid(layer_input, output_grad, gate_weight, up_weight, down_weight):
    chips = 8
    rows, tokens = layer_input.shape
    hidden, features = gate_weight.shape
    width = 2 * rows
    half = rows // 2
    bf16, f32 = jnp.bfloat16, jnp.float32
    anywhere = pl.BlockSpec(memory_space=pl.ANY)
    vmem = pl.BlockSpec(memory_space=pltpu.VMEM)
    DMA = pltpu.SemaphoreType.DMA
    VMEM = pltpu.VMEM
    small = jax.ShapeDtypeStruct((hidden, tokens), bf16)
    turned, hact, ggp, gup, gathered = pl.pallas_call(
        grid_kernel,
        out_shape=(
            jax.ShapeDtypeStruct((2 * tokens, half), bf16),
            small, small, small,
            jax.ShapeDtypeStruct((2, chips, 2, rows, tokens), bf16),
        ),
        in_specs=[anywhere] * 5,
        out_specs=(vmem, anywhere, anywhere, anywhere, anywhere),
        scratch_shapes=[
            VMEM((chips, 2, 2, rows, tokens), bf16),
            VMEM((chips, 2, hidden, width), bf16),
            VMEM((3, hidden, width), bf16),
            VMEM((3, hidden, tokens), f32),
            VMEM((hidden, tokens), bf16),
            VMEM((hidden, tokens), bf16),
            VMEM((hidden, tokens), bf16),
            VMEM((tokens, hidden), bf16),
            VMEM((tokens, hidden), bf16),
            VMEM((chips, 2 * tokens, half), f32),
            VMEM((chips, 2 * tokens, half), bf16),
            VMEM((chips, 2 * tokens, half), bf16),
            VMEM((4, 2 * tokens, half), bf16),
            VMEM((2, chips, 2 * tokens, half), bf16),
            DMA((2,)),
            DMA((3, 2)),
            DMA((4, chips, 2)),
            DMA((chips, 2, 2)),
            DMA((2, chips)),
            DMA((3,)),
            DMA((chips, 2)),
            DMA((chips, 2)),
            DMA((chips, 2)),
            DMA((4, 2)),
            DMA((2, chips, 2)),
        ],
        compiler_params=pltpu.CompilerParams(
            collective_id=0, has_side_effects=True, vmem_limit_bytes=GRID_VMEM
        ),
        name="gather_scatter",
    )(layer_input, output_grad, gate_weight, up_weight, down_weight)
    gathered = gathered.reshape(2, features, tokens)
    block = 1024

    def fixed(shape):
        return pl.BlockSpec(shape, lambda j: (0, 0))

    grads = jax.ShapeDtypeStruct((hidden, features), bf16)
    columns = pl.BlockSpec((hidden, block), lambda j: (0, j))
    gate_grad, up_grad, down_grad, input_grad = pl.pallas_call(
        weight_grads_kernel,
        grid=(features // block,),
        out_shape=(grads, grads, grads, jax.ShapeDtypeStruct((rows, tokens), bf16)),
        in_specs=[
            fixed((hidden, tokens)),
            fixed((hidden, tokens)),
            fixed((hidden, tokens)),
            pl.BlockSpec((1, block, tokens), lambda j: (0, j, 0)),
            pl.BlockSpec((1, block, tokens), lambda j: (1, j, 0)),
            fixed((2 * tokens, half)),
        ],
        out_specs=(columns, columns, columns, fixed((rows, tokens))),
        compiler_params=pltpu.CompilerParams(vmem_limit_bytes=VMEM_LIMIT),
        name="weight_grads",
    )(hact, ggp, gup, gathered, gathered, turned)
    return (input_grad, gate_grad, up_grad, down_grad)


def solution(mesh):
    row = mesh.shape["row"]
    xs = 2 if row <= 16 else 4
    zs = row // (2 * xs)
    return jax.shard_map(
        on_grid if (zs, xs) == (4, 2) else functools.partial(on_device, zs, xs),
        mesh=mesh,
        in_specs=(
            P("row", "groups"),
            P("row", "groups"),
            P(("groups", "row"), None),
            P(("groups", "row"), None),
            P(("groups", "row"), None),
        ),
        out_specs=(
            P("row", "groups"),
            P(("groups", "row"), None),
            P(("groups", "row"), None),
            P(("groups", "row"), None),
        ),
        check_vma=False,
    )
```

```python
import functools

import jax
import jax.numpy as jnp
from jax import lax
from jax.experimental import pallas as pl
from jax.experimental.pallas import tpu as pltpu
from jax.sharding import PartitionSpec as P

MESH = pl.DeviceIdType.MESH
VMEM_LIMIT = 64 * 1000 * 1000
GRID_VMEM = 64 * 1024 * 1024


def over_tokens(first_mat, second_mat):
    return lax.dot_general(
        first_mat, second_mat, (((1,), (1,)), ((), ())), preferred_element_type=jnp.float32
    )


def nearest(rank, here, extent):
    low = jnp.minimum(here, extent - 1 - here)
    half = (rank + 1) // 2
    both = jnp.where(rank % 2 == 1, here + half, here - half)
    one = jnp.where(here < extent - 1 - here, rank, extent - 1 - rank)
    return jnp.where(rank <= 2 * low, both, one)


def place(zs, xs):
    me = lax.axis_index("row")
    core = me % 2
    x = (me // 2) % xs
    z = me // (2 * xs)
    return z, x, core


def chip_at(step, z, x, zs, xs):
    if xs == 2:
        inner = (step > 0) & (step < 2 * zs - 1)
        beside = jnp.where(inner, (step + 1) % 2, jnp.minimum(step, 1))
        rank = jnp.where(inner, (step + 1) // 2 - beside, step // 2)
    else:
        rank, beside = step // xs, step % xs
    cz = nearest(rank, z, zs)
    cx = nearest(beside, x, xs)
    return cz, cx, cz * xs + cx


def greet(z, x, core, zs, xs):
    barrier = pltpu.get_barrier_semaphore()

    def hail(cz, cx, cc):
        pl.semaphore_signal(
            barrier, inc=1, device_id={"row": (cz * xs + cx) * 2 + cc}, device_id_type=MESH
        )

    hail(z, x, 1 - core)
    pl.when(z > 0)(lambda: hail(z - 1, x, core))
    pl.when(z < zs - 1)(lambda: hail(z + 1, x, core))
    pl.when(x > 0)(lambda: hail(z, x - 1, core))
    pl.when(x < xs - 1)(lambda: hail(z, x + 1, core))
    count = 1 + jnp.minimum(z, 1) + jnp.minimum(zs - 1 - z, 1)
    count = count + jnp.minimum(x, 1) + jnp.minimum(xs - 1 - x, 1)
    pl.semaphore_wait(barrier, count)


def forward_kernel(
    zs, xs, x_ref, dy_ref, wg_ref, wu_ref, wd_ref,
    hact_ref, ggp_ref, gup_ref, ggp_t_ref, gup_t_ref, xg_ref, dyg_ref,
    held, wbuf, acc, send_sem, recv_sem, wsem, own_sem, out_sem,
):
    z, x, core = place(zs, xs)
    mine = z * xs + x
    chips = zs * xs
    rows, hidden = held.shape[3], acc.shape[1]
    width = 2 * rows
    tokens = held.shape[4]

    def weights(step, fn):
        _, _, chip = chip_at(step, z, x, zs, xs)
        cols = pl.ds(pl.multiple_of(chip * width, 128), width)
        slot = step % 2
        for n, ref in enumerate((wg_ref, wu_ref, wd_ref)):
            fn(pltpu.make_async_copy(ref.at[:, cols], wbuf.at[slot, n], wsem.at[slot, n]))

    weights(0, lambda c: c.start())
    own = [
        pltpu.make_async_copy(ref, held.at[mine, n, core], own_sem.at[n])
        for n, ref in enumerate((x_ref, dy_ref))
    ]
    for c in own:
        c.start()
    greet(z, x, core, zs, xs)
    for c in own:
        c.wait()

    def passing(step, fn):
        cz, cx, chip = chip_at(step, z, x, zs, xs)
        block = held.at[chip, :, core]

        def copy(tz, tx, tc, n):
            return lambda: fn(
                pltpu.make_async_remote_copy(
                    src_ref=block,
                    dst_ref=block,
                    send_sem=send_sem.at[n, chip],
                    recv_sem=recv_sem.at[chip, core],
                    device_id={"row": (tz * xs + tx) * 2 + tc},
                    device_id_type=MESH,
                )
            )

        pl.when((cx == x) & (cz <= z) & (z < zs - 1))(copy(z + 1, x, core, 0))
        pl.when((cx == x) & (cz >= z) & (z > 0))(copy(z - 1, x, core, 1))
        pl.when((cx <= x) & (x < xs - 1))(copy(z, x + 1, core, 2))
        pl.when((cx >= x) & (x > 0))(copy(z, x - 1, core, 3))
        copy(z, x, 1 - core, 4)()

    def arrive(step, which):
        _, _, chip = chip_at(step, z, x, zs, xs)
        block = held.at[chip, :, which]
        pltpu.make_async_copy(block, block, recv_sem.at[chip, which]).wait()

    passing(0, lambda c: c.start())
    acc[...] = jnp.zeros_like(acc)

    def body(step, carry):
        @pl.when(step + 1 < chips)
        def _():
            weights(step + 1, lambda c: c.start())
            arrive(step + 1, core)
            passing(step + 1, lambda c: c.start())

        arrive(step, 1 - core)
        weights(step, lambda c: c.wait())
        _, _, chip = chip_at(step, z, x, zs, xs)
        for n, ref in enumerate((xg_ref, dyg_ref)):
            pltpu.make_async_copy(held.at[chip, n], ref.at[chip], out_sem.at[n, chip]).start()
        slot = step % 2
        x_block = held[chip, 0].reshape(width, tokens)
        acc[0] += jnp.dot(wbuf[slot, 0], x_block, preferred_element_type=jnp.float32)
        acc[1] += jnp.dot(wbuf[slot, 1], x_block, preferred_element_type=jnp.float32)
        dy_block = held[chip, 1].reshape(width, tokens)
        acc[2] += jnp.dot(wbuf[slot, 2], dy_block, preferred_element_type=jnp.float32)
        return carry

    lax.fori_loop(0, chips, body, 0)

    part = 128 if hidden % 128 == 0 else hidden
    for start in range(0, hidden, part):
        at = slice(start, start + part)
        gate_pre, up_pre, hidden_grad = acc[0, at], acc[1, at], acc[2, at]
        sig = jax.nn.sigmoid(gate_pre)
        act = gate_pre * sig
        hact_ref[at] = (act * up_pre).astype(jnp.bfloat16)
        grad_gate_pre = hidden_grad * up_pre * sig * (1.0 + gate_pre * (1.0 - sig))
        ggp_ref[at] = grad_gate_pre.astype(jnp.bfloat16)
        ggp_t_ref[:, at] = grad_gate_pre.T.astype(jnp.bfloat16)
        grad_up_pre = hidden_grad * act
        gup_ref[at] = grad_up_pre.astype(jnp.bfloat16)
        gup_t_ref[:, at] = grad_up_pre.T.astype(jnp.bfloat16)

    def drain(step, carry):
        _, _, chip = chip_at(step, z, x, zs, xs)
        passing(step, lambda c: c.wait_send())
        for n, ref in enumerate((xg_ref, dyg_ref)):
            pltpu.make_async_copy(held.at[chip, n], ref.at[chip], out_sem.at[n, chip]).wait()
        return carry

    lax.fori_loop(0, chips, drain, 0)


def scatter_kernel(
    zs, xs, ggp_ref, gup_ref, wg_ref, wu_ref, out_ref,
    wbuf, part, core_out, core_in, line_out, x_in, z_in,
    wsem, core_send, core_recv, line_send, x_recv, z_recv,
):
    z, x, core = place(zs, xs)
    chips = zs * xs
    rows, tokens = out_ref.shape
    width = 2 * rows

    def chip_of(step):
        return chip_at(chips - 1 - step, z, x, zs, xs)

    def weights(step, fn):
        _, _, chip = chip_of(step)
        cols = pl.ds(pl.multiple_of(chip * width, 128), width)
        slot = step % 2
        for n, ref in enumerate((wg_ref, wu_ref)):
            fn(pltpu.make_async_copy(ref.at[:, cols], wbuf.at[slot, n], wsem.at[slot, n]))

    def to_core(chip):
        return pltpu.make_async_remote_copy(
            src_ref=core_out.at[chip],
            dst_ref=core_in.at[chip],
            send_sem=core_send.at[chip],
            recv_sem=core_recv.at[chip],
            device_id={"row": (z * xs + x) * 2 + 1 - core},
            device_id_type=MESH,
        )

    def line(chip, tz, tx, buf, sems, side):
        return pltpu.make_async_remote_copy(
            src_ref=line_out.at[chip],
            dst_ref=buf.at[side, chip],
            send_sem=line_send.at[chip],
            recv_sem=sems.at[side, chip],
            device_id={"row": (tz * xs + tx) * 2 + core},
            device_id_type=MESH,
        )

    def onward(cz, cx, chip, fn):
        pl.when(cx > x)(lambda: fn(line(chip, z, x + 1, x_in, x_recv, 0)))
        pl.when(cx < x)(lambda: fn(line(chip, z, x - 1, x_in, x_recv, 1)))
        pl.when((cx == x) & (cz > z))(lambda: fn(line(chip, z + 1, x, z_in, z_recv, 0)))
        pl.when((cx == x) & (cz < z))(lambda: fn(line(chip, z - 1, x, z_in, z_recv, 1)))

    weights(0, lambda c: c.start())
    greet(z, x, core, zs, xs)

    def make(step):
        slot = step % 2
        _, _, chip = chip_of(step)

        @pl.when(step + 1 < chips)
        def _():
            weights(step + 1, lambda c: c.start())

        weights(step, lambda c: c.wait())
        total = jnp.dot(ggp_ref[...], wbuf[slot, 0], preferred_element_type=jnp.float32)
        total += jnp.dot(gup_ref[...], wbuf[slot, 1], preferred_element_type=jnp.float32)
        part[slot] = total.T.reshape(2, rows, tokens)
        core_out[chip] = part[slot, 1 - core].astype(jnp.bfloat16)
        to_core(chip).start()

    def add(step):
        slot = step % 2
        cz, cx, chip = chip_of(step)
        to_core(chip).wait_recv()
        part[slot, core] += core_in[chip].astype(jnp.float32)

        def take(buf, sems, side):
            def run():
                block = buf.at[side, chip]
                pltpu.make_async_copy(block, block, sems.at[side, chip]).wait()
                part[slot, core] += buf[side, chip].astype(jnp.float32)

            return run

        pl.when((cx >= x) & (x > 0))(take(x_in, x_recv, 0))
        pl.when((cx <= x) & (x < xs - 1))(take(x_in, x_recv, 1))
        pl.when((cx == x) & (cz >= z) & (z > 0))(take(z_in, z_recv, 0))
        pl.when((cx == x) & (cz <= z) & (z < zs - 1))(take(z_in, z_recv, 1))
        line_out[chip] = part[slot, core].astype(jnp.bfloat16)
        onward(cz, cx, chip, lambda c: c.start())

    make(0)

    def body(step, carry):
        make(step)
        add(step - 1)
        return carry

    lax.fori_loop(1, chips, body, 0)
    add(chips - 1)
    out_ref[...] = line_out[z * xs + x]

    def drain(step, carry):
        cz, cx, chip = chip_of(step)
        to_core(chip).wait_send()
        onward(cz, cx, chip, lambda c: c.wait_send())
        return carry

    lax.fori_loop(0, chips, drain, 0)


def on_device(zs, xs, layer_input, output_grad, gate_weight, up_weight, down_weight):
    chips = zs * xs
    rows, tokens = layer_input.shape
    hidden, features = gate_weight.shape
    width = 2 * rows
    bf16, f32 = jnp.bfloat16, jnp.float32
    anywhere = pl.BlockSpec(memory_space=pl.ANY)
    vmem = pl.BlockSpec(memory_space=pltpu.VMEM)
    DMA = pltpu.SemaphoreType.DMA
    small = jax.ShapeDtypeStruct((hidden, tokens), bf16)
    turned = jax.ShapeDtypeStruct((tokens, hidden), bf16)
    whole = jax.ShapeDtypeStruct((chips, 2, rows, tokens), bf16)
    hidden_act, ggp, gup, ggp_t, gup_t, xg, dyg = pl.pallas_call(
        functools.partial(forward_kernel, zs, xs),
        out_shape=(small, small, small, turned, turned, whole, whole),
        in_specs=[anywhere] * 5,
        out_specs=(vmem, vmem, vmem, vmem, vmem, anywhere, anywhere),
        scratch_shapes=[
            pltpu.VMEM((chips, 2, 2, rows, tokens), bf16),
            pltpu.VMEM((2, 3, hidden, width), bf16),
            pltpu.VMEM((3, hidden, tokens), f32),
            DMA((5, chips)),
            DMA((chips, 2)),
            DMA((2, 3)),
            DMA((2,)),
            DMA((2, chips)),
        ],
        compiler_params=pltpu.CompilerParams(
            collective_id=0, has_side_effects=True, vmem_limit_bytes=VMEM_LIMIT
        ),
        name="gather_forward",
    )(layer_input, output_grad, gate_weight, up_weight, down_weight)
    input_grad = pl.pallas_call(
        functools.partial(scatter_kernel, zs, xs),
        out_shape=jax.ShapeDtypeStruct((rows, tokens), bf16),
        in_specs=[vmem, vmem, anywhere, anywhere],
        out_specs=vmem,
        scratch_shapes=[
            pltpu.VMEM((2, 2, hidden, width), bf16),
            pltpu.VMEM((2, 2, rows, tokens), f32),
            pltpu.VMEM((chips, rows, tokens), bf16),
            pltpu.VMEM((chips, rows, tokens), bf16),
            pltpu.VMEM((chips, rows, tokens), bf16),
            pltpu.VMEM((2, chips, rows, tokens), bf16),
            pltpu.VMEM((2, chips, rows, tokens), bf16),
            DMA((2, 2)),
            DMA((chips,)),
            DMA((chips,)),
            DMA((chips,)),
            DMA((2, chips)),
            DMA((2, chips)),
        ],
        compiler_params=pltpu.CompilerParams(
            collective_id=1, has_side_effects=True, vmem_limit_bytes=VMEM_LIMIT
        ),
        name="scatter_input_grad",
    )(ggp_t, gup_t, gate_weight, up_weight)
    block_in = xg.reshape(features, tokens)
    block_dy = dyg.reshape(features, tokens)
    down_grad = over_tokens(hidden_act, block_dy).astype(bf16)
    gate_grad = over_tokens(ggp, block_in).astype(bf16)
    up_grad = over_tokens(gup, block_in).astype(bf16)
    return (input_grad, gate_grad, up_grad, down_grad)


EVENTS = (
    (16, 17, 5, 4, 18, 19, 8, 3, 20, 21, 12, 6, 9, 2, 22, 23, 24, 25, 14, 10, 13, 7, 26, 27, 32, 28, 15, 29,
     11, 30, 31),
    (16, 17, 0, 8, 6, 18, 19, 20, 7, 1, 9, 21, 22, 23, 12, 24, 10, 2, 25, 3, 13, 26, 27, 28, 15, 11, 29, 14,
     30, 31, 32),
)
USE = (
    (0, 1, 5, 4, 8, 3, 12, 2, 6, 9, 14, 10, 7, 13, 15, 11),
    (4, 5, 0, 6, 8, 7, 1, 9, 12, 10, 2, 3, 13, 15, 11, 14),
)
GIVE = (
    (7, 5, 22, 23, 6, 18, 19, 4, 21, 0, 20, 3, 1, 14, 16, 15, 2, 10, 17, 12, 11, 13, 8, 9),
    (1, 7, 10, 6, 22, 5, 4, 18, 19, 3, 0, 14, 15, 2, 23, 21, 11, 20, 9, 16, 8, 17, 12, 13),
)


def listed(rows, inside):
    return [jnp.where(inside, b, a) for a, b in zip(*rows)]


def entry(values, step):
    found = values[0]
    for n, value in enumerate(values[1:], 1):
        found = jnp.where(step == n, value, found)
    return found


def grid_kernel(
    x_ref, dy_ref, wg_ref, wu_ref, wd_ref,
    grad_ref, hact_ref, pre_ref, all_ref,
    held, wgu, wdn, acc, hact, ggp, gup, turned, part, outb, core_in, x_in, z_in,
    own_sem, wsem, send_sem, recv_sem, all_sem, small_sem,
    core_send, core_recv, line_send, x_recv, z_recv,
):
    zs, xs = 4, 2
    z, x, core = place(zs, xs)
    mine = z * xs + x
    rows, hidden, tokens = held.shape[3], acc.shape[1], acc.shape[2]
    width = 2 * rows
    half = rows // 2
    low = z < 2
    inside = (z > 0) & (z < 3)
    events = listed(EVENTS, inside)
    use = listed(USE, inside)
    give = listed(GIVE, inside)
    f32, bf16 = jnp.float32, jnp.bfloat16

    def target(cz, cx, cc):
        return {"row": (cz * xs + cx) * 2 + cc}

    def piece_at(code):
        near = code // 4
        cz = jnp.where(low, near, 3 - near)
        cx = jnp.where((code // 2) % 2 == 1, 1 - x, x)
        return cz, cx, cz * xs + cx, code % 2

    def weights(step, fn):
        _, _, chip, n = piece_at(entry(use, step))
        slot = step % 3
        cols = pl.ds(pl.multiple_of(chip * width, 128), width)

        @pl.when(n == 0)
        def _():
            fn(pltpu.make_async_copy(wg_ref.at[:, cols], wgu.at[chip, :hidden], wsem.at[slot, 0]))
            fn(pltpu.make_async_copy(wu_ref.at[:, cols], wgu.at[chip, hidden:], wsem.at[slot, 1]))

        @pl.when(n == 1)
        def _():
            fn(pltpu.make_async_copy(wd_ref.at[:, cols], wdn.at[slot], wsem.at[slot, 0]))

    def passing(cz, cx, chip, n, src, fn):
        two = ((cz == 0) | (cz == zs - 1)) & (n == 1)
        column = cx == x
        along = column | two

        def copy(tz, tx, tc, way):
            return lambda: fn(
                pltpu.make_async_remote_copy(
                    src_ref=src,
                    dst_ref=held.at[chip, n, core],
                    send_sem=send_sem.at[way, chip, n],
                    recv_sem=recv_sem.at[chip, n, core],
                    device_id=target(tz, tx, tc),
                    device_id_type=MESH,
                )
            )

        pl.when(along & (cz <= z) & (z < zs - 1))(copy(z + 1, x, core, 0))
        pl.when(along & (cz >= z) & (z > 0))(copy(z - 1, x, core, 1))
        pl.when(column & (jnp.logical_not(two) | (cz == z)))(copy(z, 1 - x, core, 2))
        copy(z, x, 1 - core, 3)()

    def arrive(chip, n, which):
        block = held.at[chip, n, which]
        pltpu.make_async_copy(block, block, recv_sem.at[chip, n, which]).wait()

    own = [
        pltpu.make_async_copy(ref, held.at[mine, n, core], own_sem.at[n])
        for n, ref in enumerate((x_ref, dy_ref))
    ]
    for c in own:
        c.start()
    greet(z, x, core, zs, xs)
    for n, ref in enumerate((x_ref, dy_ref)):
        passing(z, x, mine, n, ref, lambda c: c.start())
    weights(0, lambda c: c.start())
    weights(1, lambda c: c.start())
    acc[...] = jnp.zeros_like(acc)
    for c in own:
        c.wait()

    part_rows = 128 if hidden % 128 == 0 else hidden

    def gather(step, carry):
        event = entry(events, step)

        @pl.when(event < 16)
        def _():
            cz, cx, chip, n = piece_at(event)
            arrive(chip, n, core)
            passing(cz, cx, chip, n, held.at[chip, n, core], lambda c: c.start())

        @pl.when((event >= 16) & (event < 32))
        def _():
            count = event - 16
            cz, cx, chip, n = piece_at(entry(use, count))
            pl.when(count + 2 < 16)(lambda: weights(count + 2, lambda c: c.start()))
            arrive(chip, n, 1 - core)
            pltpu.make_async_copy(held.at[chip, n], all_ref.at[n, chip], all_sem.at[n, chip]).start()
            weights(count, lambda c: c.wait())

            @pl.when(n == 0)
            def _():
                block = held[chip, 0].reshape(width, tokens)
                acc[0] += jnp.dot(wgu[chip, :hidden], block, preferred_element_type=f32)
                acc[1] += jnp.dot(wgu[chip, hidden:], block, preferred_element_type=f32)

            @pl.when(n == 1)
            def _():
                block = held[chip, 1].reshape(width, tokens)
                acc[2] += jnp.dot(wdn[count % 3], block, preferred_element_type=f32)

        @pl.when(event == 32)
        def _():
            for start in range(0, hidden, part_rows):
                at = slice(start, start + part_rows)
                gate_pre, up_pre = acc[0, at], acc[1, at]
                sig = jax.nn.sigmoid(gate_pre)
                act = gate_pre * sig
                hact[at] = (act * up_pre).astype(bf16)
                acc[0, at] = up_pre * sig * (1.0 + gate_pre * (1.0 - sig))
                acc[1, at] = act

        return carry

    lax.fori_loop(0, len(EVENTS[0]), gather, 0)

    for start in range(0, hidden, part_rows):
        at = slice(start, start + part_rows)
        hidden_grad = acc[2, at]
        grad_gate_pre = (hidden_grad * acc[0, at]).astype(bf16)
        grad_up_pre = (hidden_grad * acc[1, at]).astype(bf16)
        ggp[at] = grad_gate_pre
        turned[:, at] = grad_gate_pre.T
        gup[at] = grad_up_pre
        turned[:, hidden + start : hidden + start + part_rows] = grad_up_pre.T
    small = [
        pltpu.make_async_copy(src, dst, small_sem.at[n])
        for n, (src, dst) in enumerate(((hact, hact_ref), (ggp, pre_ref.at[0]), (gup, pre_ref.at[1])))
    ]
    for c in small:
        c.start()

    def to_core(chip, h):
        at = pl.ds(pl.multiple_of(h * tokens, tokens), tokens)
        return pltpu.make_async_remote_copy(
            src_ref=outb.at[chip, at],
            dst_ref=core_in.at[chip, at],
            send_sem=core_send.at[chip, h],
            recv_sem=core_recv.at[chip, h],
            device_id=target(z, x, 1 - core),
            device_id_type=MESH,
        )

    def onward(cz, cx, chip, h, fn):
        two = ((cz == 0) | (cz == zs - 1)) & (h == 1)
        along = (cx == x) | two
        at = pl.ds(pl.multiple_of(h * tokens, tokens), tokens)

        def line(tz, tx, dst, sem):
            return lambda: fn(
                pltpu.make_async_remote_copy(
                    src_ref=outb.at[chip, at],
                    dst_ref=dst,
                    send_sem=line_send.at[chip, h],
                    recv_sem=sem,
                    device_id=target(tz, tx, core),
                    device_id_type=MESH,
                )
            )

        pl.when(along & (cz > z))(line(z + 1, x, z_in.at[0, chip, at], z_recv.at[0, chip, h]))
        pl.when(along & (cz < z))(line(z - 1, x, z_in.at[1, chip, at], z_recv.at[1, chip, h]))
        pl.when((cx != x) & (jnp.logical_not(two) | (cz == z)))(
            line(z, 1 - x, x_in.at[cz, at], x_recv.at[cz, h])
        )

    def block_at(code):
        near = code // 2
        cz = jnp.where(low, near, 3 - near)
        cx = jnp.where(code % 2 == 1, 1 - x, x)
        return cz, cx, cz * xs + cx

    def scatter(step, carry):
        code = entry(give, step)

        @pl.when(code < 8)
        def _():
            _, _, chip = block_at(code)

            def product(which):
                cols = pl.ds(pl.multiple_of(which * rows, 128), rows)
                return jnp.dot(turned[...], wgu[chip, :, cols], preferred_element_type=f32)

            total = product(1 - core)
            for h in range(2):
                at = slice(h * tokens, (h + 1) * tokens)
                outb[chip, at] = total[:, h * half : (h + 1) * half].astype(bf16)
                to_core(chip, h).start()
            total = product(core)
            for h in range(2):
                at = slice(h * tokens, (h + 1) * tokens)
                part[chip, at] = total[:, h * half : (h + 1) * half]

        @pl.when(code >= 8)
        def _():
            h = code % 2
            cz, cx, chip = block_at((code - 8) // 2)
            two = ((cz == 0) | (cz == zs - 1)) & (h == 1)
            along = (cx == x) | two
            at = pl.ds(pl.multiple_of(h * tokens, tokens), tokens)
            to_core(chip, h).wait()
            part[chip, at] += core_in[chip, at].astype(f32)

            def gain(block, sem):
                def run():
                    pltpu.make_async_copy(block, block, sem).wait()
                    part[chip, at] += block[...].astype(f32)

                return run

            pl.when((cx == x) & (jnp.logical_not(two) | (cz == z)))(
                gain(x_in.at[cz, at], x_recv.at[cz, h])
            )
            pl.when(along & (cz >= z) & (z > 0))(gain(z_in.at[0, chip, at], z_recv.at[0, chip, h]))
            pl.when(along & (cz <= z) & (z < zs - 1))(
                gain(z_in.at[1, chip, at], z_recv.at[1, chip, h])
            )
            outb[chip, at] = part[chip, at].astype(bf16)
            onward(cz, cx, chip, h, lambda c: c.start())

        return carry

    lax.fori_loop(0, len(GIVE[0]), scatter, 0)
    for h in range(2):
        grad_ref[h * half : (h + 1) * half] = outb[mine, h * tokens : (h + 1) * tokens].T

    for c in small:
        c.wait()

    def drain(step, carry):
        cz, cx, chip, n = piece_at(step)
        passing(cz, cx, chip, n, held.at[chip, n, core], lambda c: c.wait_send())
        pltpu.make_async_copy(held.at[chip, n], all_ref.at[n, chip], all_sem.at[n, chip]).wait()
        onward(cz, cx, chip, n, lambda c: c.wait_send())
        return carry

    lax.fori_loop(0, 16, drain, 0)


def weight_grads_kernel(
    hact_ref, pre_ref, x_ref, dy_ref, gate_ref, up_ref, down_ref
):
    bf16 = jnp.bfloat16
    hidden = gate_ref.shape[0]
    both = over_tokens(pre_ref[...], x_ref[0]).astype(bf16)
    gate_ref[...] = both[:hidden]
    up_ref[...] = both[hidden:]
    down_ref[...] = over_tokens(hact_ref[...], dy_ref[0]).astype(bf16)


def on_grid(layer_input, output_grad, gate_weight, up_weight, down_weight):
    chips = 8
    rows, tokens = layer_input.shape
    hidden, features = gate_weight.shape
    width = 2 * rows
    half = rows // 2
    bf16, f32 = jnp.bfloat16, jnp.float32
    anywhere = pl.BlockSpec(memory_space=pl.ANY)
    vmem = pl.BlockSpec(memory_space=pltpu.VMEM)
    DMA = pltpu.SemaphoreType.DMA
    VMEM = pltpu.VMEM
    small = jax.ShapeDtypeStruct((hidden, tokens), bf16)
    grad, hact, pre, gathered = pl.pallas_call(
        grid_kernel,
        out_shape=(
            jax.ShapeDtypeStruct((rows, tokens), bf16),
            small, jax.ShapeDtypeStruct((2, hidden, tokens), bf16),
            jax.ShapeDtypeStruct((2, chips, 2, rows, tokens), bf16),
        ),
        in_specs=[anywhere] * 5,
        out_specs=(vmem, anywhere, anywhere, anywhere),
        scratch_shapes=[
            VMEM((chips, 2, 2, rows, tokens), bf16),
            VMEM((chips, 2 * hidden, width), bf16),
            VMEM((3, hidden, width), bf16),
            VMEM((3, hidden, tokens), f32),
            VMEM((hidden, tokens), bf16),
            VMEM((hidden, tokens), bf16),
            VMEM((hidden, tokens), bf16),
            VMEM((tokens, 2 * hidden), bf16),
            VMEM((chips, 2 * tokens, half), f32),
            VMEM((chips, 2 * tokens, half), bf16),
            VMEM((chips, 2 * tokens, half), bf16),
            VMEM((4, 2 * tokens, half), bf16),
            VMEM((2, chips, 2 * tokens, half), bf16),
            DMA((2,)),
            DMA((3, 2)),
            DMA((4, chips, 2)),
            DMA((chips, 2, 2)),
            DMA((2, chips)),
            DMA((3,)),
            DMA((chips, 2)),
            DMA((chips, 2)),
            DMA((chips, 2)),
            DMA((4, 2)),
            DMA((2, chips, 2)),
        ],
        compiler_params=pltpu.CompilerParams(
            collective_id=0, has_side_effects=True, vmem_limit_bytes=GRID_VMEM
        ),
        name="gather_scatter",
    )(layer_input, output_grad, gate_weight, up_weight, down_weight)
    gathered = gathered.reshape(2, features, tokens)
    block = 1024

    def fixed(shape):
        return pl.BlockSpec(shape, lambda j: (0, 0))

    grads = jax.ShapeDtypeStruct((hidden, features), bf16)
    columns = pl.BlockSpec((hidden, block), lambda j: (0, j))
    gate_grad, up_grad, down_grad = pl.pallas_call(
        weight_grads_kernel,
        grid=(features // block,),
        out_shape=(grads, grads, grads),
        in_specs=[
            fixed((hidden, tokens)),
            fixed((2 * hidden, tokens)),
            pl.BlockSpec((1, block, tokens), lambda j: (0, j, 0)),
            pl.BlockSpec((1, block, tokens), lambda j: (1, j, 0)),
        ],
        out_specs=(columns, columns, columns),
        compiler_params=pltpu.CompilerParams(vmem_limit_bytes=VMEM_LIMIT),
        name="weight_grads",
    )(hact, pre.reshape(2 * hidden, tokens), gathered, gathered)
    return (grad, gate_grad, up_grad, down_grad)


def solution(mesh):
    row = mesh.shape["row"]
    xs = 2 if row <= 16 else 4
    zs = row // (2 * xs)
    return jax.shard_map(
        on_grid if (zs, xs) == (4, 2) else functools.partial(on_device, zs, xs),
        mesh=mesh,
        in_specs=(
            P("row", "groups"),
            P("row", "groups"),
            P(("groups", "row"), None),
            P(("groups", "row"), None),
            P(("groups", "row"), None),
        ),
        out_specs=(
            P("row", "groups"),
            P(("groups", "row"), None),
            P(("groups", "row"), None),
            P(("groups", "row"), None),
        ),
        check_vma=False,
    )
```

```python
import functools

import jax
import jax.numpy as jnp
from jax import lax
from jax.experimental import pallas as pl
from jax.experimental.pallas import tpu as pltpu
from jax.sharding import PartitionSpec as P

MESH = pl.DeviceIdType.MESH
VMEM_LIMIT = 64 * 1000 * 1000
GRID_VMEM = 64 * 1024 * 1024


def over_tokens(first_mat, second_mat):
    return lax.dot_general(
        first_mat, second_mat, (((1,), (1,)), ((), ())), preferred_element_type=jnp.float32
    )


def nearest(rank, here, extent):
    low = jnp.minimum(here, extent - 1 - here)
    half = (rank + 1) // 2
    both = jnp.where(rank % 2 == 1, here + half, here - half)
    one = jnp.where(here < extent - 1 - here, rank, extent - 1 - rank)
    return jnp.where(rank <= 2 * low, both, one)


def place(zs, xs):
    me = lax.axis_index("row")
    core = me % 2
    x = (me // 2) % xs
    z = me // (2 * xs)
    return z, x, core


def chip_at(step, z, x, zs, xs):
    if xs == 2:
        inner = (step > 0) & (step < 2 * zs - 1)
        beside = jnp.where(inner, (step + 1) % 2, jnp.minimum(step, 1))
        rank = jnp.where(inner, (step + 1) // 2 - beside, step // 2)
    else:
        rank, beside = step // xs, step % xs
    cz = nearest(rank, z, zs)
    cx = nearest(beside, x, xs)
    return cz, cx, cz * xs + cx


def greet(z, x, core, zs, xs):
    barrier = pltpu.get_barrier_semaphore()

    def hail(cz, cx, cc):
        pl.semaphore_signal(
            barrier, inc=1, device_id={"row": (cz * xs + cx) * 2 + cc}, device_id_type=MESH
        )

    hail(z, x, 1 - core)
    pl.when(z > 0)(lambda: hail(z - 1, x, core))
    pl.when(z < zs - 1)(lambda: hail(z + 1, x, core))
    pl.when(x > 0)(lambda: hail(z, x - 1, core))
    pl.when(x < xs - 1)(lambda: hail(z, x + 1, core))
    count = 1 + jnp.minimum(z, 1) + jnp.minimum(zs - 1 - z, 1)
    count = count + jnp.minimum(x, 1) + jnp.minimum(xs - 1 - x, 1)
    pl.semaphore_wait(barrier, count)


def forward_kernel(
    zs, xs, x_ref, dy_ref, wg_ref, wu_ref, wd_ref,
    hact_ref, ggp_ref, gup_ref, ggp_t_ref, gup_t_ref, xg_ref, dyg_ref,
    held, wbuf, acc, send_sem, recv_sem, wsem, own_sem, out_sem,
):
    z, x, core = place(zs, xs)
    mine = z * xs + x
    chips = zs * xs
    rows, hidden = held.shape[3], acc.shape[1]
    width = 2 * rows
    tokens = held.shape[4]

    def weights(step, fn):
        _, _, chip = chip_at(step, z, x, zs, xs)
        cols = pl.ds(pl.multiple_of(chip * width, 128), width)
        slot = step % 2
        for n, ref in enumerate((wg_ref, wu_ref, wd_ref)):
            fn(pltpu.make_async_copy(ref.at[:, cols], wbuf.at[slot, n], wsem.at[slot, n]))

    weights(0, lambda c: c.start())
    own = [
        pltpu.make_async_copy(ref, held.at[mine, n, core], own_sem.at[n])
        for n, ref in enumerate((x_ref, dy_ref))
    ]
    for c in own:
        c.start()
    greet(z, x, core, zs, xs)
    for c in own:
        c.wait()

    def passing(step, fn):
        cz, cx, chip = chip_at(step, z, x, zs, xs)
        block = held.at[chip, :, core]

        def copy(tz, tx, tc, n):
            return lambda: fn(
                pltpu.make_async_remote_copy(
                    src_ref=block,
                    dst_ref=block,
                    send_sem=send_sem.at[n, chip],
                    recv_sem=recv_sem.at[chip, core],
                    device_id={"row": (tz * xs + tx) * 2 + tc},
                    device_id_type=MESH,
                )
            )

        pl.when((cx == x) & (cz <= z) & (z < zs - 1))(copy(z + 1, x, core, 0))
        pl.when((cx == x) & (cz >= z) & (z > 0))(copy(z - 1, x, core, 1))
        pl.when((cx <= x) & (x < xs - 1))(copy(z, x + 1, core, 2))
        pl.when((cx >= x) & (x > 0))(copy(z, x - 1, core, 3))
        copy(z, x, 1 - core, 4)()

    def arrive(step, which):
        _, _, chip = chip_at(step, z, x, zs, xs)
        block = held.at[chip, :, which]
        pltpu.make_async_copy(block, block, recv_sem.at[chip, which]).wait()

    passing(0, lambda c: c.start())
    acc[...] = jnp.zeros_like(acc)

    def body(step, carry):
        @pl.when(step + 1 < chips)
        def _():
            weights(step + 1, lambda c: c.start())
            arrive(step + 1, core)
            passing(step + 1, lambda c: c.start())

        arrive(step, 1 - core)
        weights(step, lambda c: c.wait())
        _, _, chip = chip_at(step, z, x, zs, xs)
        for n, ref in enumerate((xg_ref, dyg_ref)):
            pltpu.make_async_copy(held.at[chip, n], ref.at[chip], out_sem.at[n, chip]).start()
        slot = step % 2
        x_block = held[chip, 0].reshape(width, tokens)
        acc[0] += jnp.dot(wbuf[slot, 0], x_block, preferred_element_type=jnp.float32)
        acc[1] += jnp.dot(wbuf[slot, 1], x_block, preferred_element_type=jnp.float32)
        dy_block = held[chip, 1].reshape(width, tokens)
        acc[2] += jnp.dot(wbuf[slot, 2], dy_block, preferred_element_type=jnp.float32)
        return carry

    lax.fori_loop(0, chips, body, 0)

    part = 128 if hidden % 128 == 0 else hidden
    for start in range(0, hidden, part):
        at = slice(start, start + part)
        gate_pre, up_pre, hidden_grad = acc[0, at], acc[1, at], acc[2, at]
        sig = jax.nn.sigmoid(gate_pre)
        act = gate_pre * sig
        hact_ref[at] = (act * up_pre).astype(jnp.bfloat16)
        grad_gate_pre = hidden_grad * up_pre * sig * (1.0 + gate_pre * (1.0 - sig))
        ggp_ref[at] = grad_gate_pre.astype(jnp.bfloat16)
        ggp_t_ref[:, at] = grad_gate_pre.T.astype(jnp.bfloat16)
        grad_up_pre = hidden_grad * act
        gup_ref[at] = grad_up_pre.astype(jnp.bfloat16)
        gup_t_ref[:, at] = grad_up_pre.T.astype(jnp.bfloat16)

    def drain(step, carry):
        _, _, chip = chip_at(step, z, x, zs, xs)
        passing(step, lambda c: c.wait_send())
        for n, ref in enumerate((xg_ref, dyg_ref)):
            pltpu.make_async_copy(held.at[chip, n], ref.at[chip], out_sem.at[n, chip]).wait()
        return carry

    lax.fori_loop(0, chips, drain, 0)


def scatter_kernel(
    zs, xs, ggp_ref, gup_ref, wg_ref, wu_ref, out_ref,
    wbuf, part, core_out, core_in, line_out, x_in, z_in,
    wsem, core_send, core_recv, line_send, x_recv, z_recv,
):
    z, x, core = place(zs, xs)
    chips = zs * xs
    rows, tokens = out_ref.shape
    width = 2 * rows

    def chip_of(step):
        return chip_at(chips - 1 - step, z, x, zs, xs)

    def weights(step, fn):
        _, _, chip = chip_of(step)
        cols = pl.ds(pl.multiple_of(chip * width, 128), width)
        slot = step % 2
        for n, ref in enumerate((wg_ref, wu_ref)):
            fn(pltpu.make_async_copy(ref.at[:, cols], wbuf.at[slot, n], wsem.at[slot, n]))

    def to_core(chip):
        return pltpu.make_async_remote_copy(
            src_ref=core_out.at[chip],
            dst_ref=core_in.at[chip],
            send_sem=core_send.at[chip],
            recv_sem=core_recv.at[chip],
            device_id={"row": (z * xs + x) * 2 + 1 - core},
            device_id_type=MESH,
        )

    def line(chip, tz, tx, buf, sems, side):
        return pltpu.make_async_remote_copy(
            src_ref=line_out.at[chip],
            dst_ref=buf.at[side, chip],
            send_sem=line_send.at[chip],
            recv_sem=sems.at[side, chip],
            device_id={"row": (tz * xs + tx) * 2 + core},
            device_id_type=MESH,
        )

    def onward(cz, cx, chip, fn):
        pl.when(cx > x)(lambda: fn(line(chip, z, x + 1, x_in, x_recv, 0)))
        pl.when(cx < x)(lambda: fn(line(chip, z, x - 1, x_in, x_recv, 1)))
        pl.when((cx == x) & (cz > z))(lambda: fn(line(chip, z + 1, x, z_in, z_recv, 0)))
        pl.when((cx == x) & (cz < z))(lambda: fn(line(chip, z - 1, x, z_in, z_recv, 1)))

    weights(0, lambda c: c.start())
    greet(z, x, core, zs, xs)

    def make(step):
        slot = step % 2
        _, _, chip = chip_of(step)

        @pl.when(step + 1 < chips)
        def _():
            weights(step + 1, lambda c: c.start())

        weights(step, lambda c: c.wait())
        total = jnp.dot(ggp_ref[...], wbuf[slot, 0], preferred_element_type=jnp.float32)
        total += jnp.dot(gup_ref[...], wbuf[slot, 1], preferred_element_type=jnp.float32)
        part[slot] = total.T.reshape(2, rows, tokens)
        core_out[chip] = part[slot, 1 - core].astype(jnp.bfloat16)
        to_core(chip).start()

    def add(step):
        slot = step % 2
        cz, cx, chip = chip_of(step)
        to_core(chip).wait_recv()
        part[slot, core] += core_in[chip].astype(jnp.float32)

        def take(buf, sems, side):
            def run():
                block = buf.at[side, chip]
                pltpu.make_async_copy(block, block, sems.at[side, chip]).wait()
                part[slot, core] += buf[side, chip].astype(jnp.float32)

            return run

        pl.when((cx >= x) & (x > 0))(take(x_in, x_recv, 0))
        pl.when((cx <= x) & (x < xs - 1))(take(x_in, x_recv, 1))
        pl.when((cx == x) & (cz >= z) & (z > 0))(take(z_in, z_recv, 0))
        pl.when((cx == x) & (cz <= z) & (z < zs - 1))(take(z_in, z_recv, 1))
        line_out[chip] = part[slot, core].astype(jnp.bfloat16)
        onward(cz, cx, chip, lambda c: c.start())

    make(0)

    def body(step, carry):
        make(step)
        add(step - 1)
        return carry

    lax.fori_loop(1, chips, body, 0)
    add(chips - 1)
    out_ref[...] = line_out[z * xs + x]

    def drain(step, carry):
        cz, cx, chip = chip_of(step)
        to_core(chip).wait_send()
        onward(cz, cx, chip, lambda c: c.wait_send())
        return carry

    lax.fori_loop(0, chips, drain, 0)


def on_device(zs, xs, layer_input, output_grad, gate_weight, up_weight, down_weight):
    chips = zs * xs
    rows, tokens = layer_input.shape
    hidden, features = gate_weight.shape
    width = 2 * rows
    bf16, f32 = jnp.bfloat16, jnp.float32
    anywhere = pl.BlockSpec(memory_space=pl.ANY)
    vmem = pl.BlockSpec(memory_space=pltpu.VMEM)
    DMA = pltpu.SemaphoreType.DMA
    small = jax.ShapeDtypeStruct((hidden, tokens), bf16)
    turned = jax.ShapeDtypeStruct((tokens, hidden), bf16)
    whole = jax.ShapeDtypeStruct((chips, 2, rows, tokens), bf16)
    hidden_act, ggp, gup, ggp_t, gup_t, xg, dyg = pl.pallas_call(
        functools.partial(forward_kernel, zs, xs),
        out_shape=(small, small, small, turned, turned, whole, whole),
        in_specs=[anywhere] * 5,
        out_specs=(vmem, vmem, vmem, vmem, vmem, anywhere, anywhere),
        scratch_shapes=[
            pltpu.VMEM((chips, 2, 2, rows, tokens), bf16),
            pltpu.VMEM((2, 3, hidden, width), bf16),
            pltpu.VMEM((3, hidden, tokens), f32),
            DMA((5, chips)),
            DMA((chips, 2)),
            DMA((2, 3)),
            DMA((2,)),
            DMA((2, chips)),
        ],
        compiler_params=pltpu.CompilerParams(
            collective_id=0, has_side_effects=True, vmem_limit_bytes=VMEM_LIMIT
        ),
        name="gather_forward",
    )(layer_input, output_grad, gate_weight, up_weight, down_weight)
    input_grad = pl.pallas_call(
        functools.partial(scatter_kernel, zs, xs),
        out_shape=jax.ShapeDtypeStruct((rows, tokens), bf16),
        in_specs=[vmem, vmem, anywhere, anywhere],
        out_specs=vmem,
        scratch_shapes=[
            pltpu.VMEM((2, 2, hidden, width), bf16),
            pltpu.VMEM((2, 2, rows, tokens), f32),
            pltpu.VMEM((chips, rows, tokens), bf16),
            pltpu.VMEM((chips, rows, tokens), bf16),
            pltpu.VMEM((chips, rows, tokens), bf16),
            pltpu.VMEM((2, chips, rows, tokens), bf16),
            pltpu.VMEM((2, chips, rows, tokens), bf16),
            DMA((2, 2)),
            DMA((chips,)),
            DMA((chips,)),
            DMA((chips,)),
            DMA((2, chips)),
            DMA((2, chips)),
        ],
        compiler_params=pltpu.CompilerParams(
            collective_id=1, has_side_effects=True, vmem_limit_bytes=VMEM_LIMIT
        ),
        name="scatter_input_grad",
    )(ggp_t, gup_t, gate_weight, up_weight)
    block_in = xg.reshape(features, tokens)
    block_dy = dyg.reshape(features, tokens)
    down_grad = over_tokens(hidden_act, block_dy).astype(bf16)
    gate_grad = over_tokens(ggp, block_in).astype(bf16)
    up_grad = over_tokens(gup, block_in).astype(bf16)
    return (input_grad, gate_grad, up_grad, down_grad)


EVENTS = (
    (16, 17, 5, 4, 18, 19, 8, 3, 20, 21, 12, 6, 9, 2, 22, 23, 24, 25, 14, 10, 13, 7, 26, 27, 32, 28, 15, 29,
     11, 30, 31),
    (16, 17, 0, 8, 6, 18, 19, 20, 7, 1, 9, 21, 22, 23, 12, 24, 10, 2, 25, 3, 13, 26, 27, 28, 15, 11, 29, 14,
     30, 31, 32),
)
USE = (
    (0, 1, 5, 4, 8, 3, 12, 2, 6, 9, 14, 10, 7, 13, 15, 11),
    (4, 5, 0, 6, 8, 7, 1, 9, 12, 10, 2, 3, 13, 15, 11, 14),
)
GIVE = (
    (7, 5, 22, 23, 6, 18, 19, 4, 21, 0, 20, 3, 1, 14, 16, 15, 2, 10, 17, 12, 11, 13, 8, 9),
    (1, 7, 10, 6, 22, 5, 4, 18, 19, 3, 0, 14, 15, 2, 23, 21, 11, 20, 9, 16, 8, 17, 12, 13),
)


def listed(rows, inside):
    return [jnp.where(inside, b, a) for a, b in zip(*rows)]


def entry(values, step):
    found = values[0]
    for n, value in enumerate(values[1:], 1):
        found = jnp.where(step == n, value, found)
    return found


def grid_kernel(
    x_ref, dy_ref, wg_ref, wu_ref, wd_ref,
    grad_ref, hact_ref, pre_ref, all_ref,
    held, wgu, wdn, acc, hact, ggp, gup, turned, part, outb, core_in, x_in, z_in,
    own_sem, wsem, send_sem, recv_sem, all_sem, small_sem,
    core_send, core_recv, line_send, x_recv, z_recv,
):
    zs, xs = 4, 2
    z, x, core = place(zs, xs)
    mine = z * xs + x
    rows, hidden, tokens = held.shape[3], acc.shape[1], acc.shape[2]
    width = 2 * rows
    half = rows // 2
    low = z < 2
    inside = (z > 0) & (z < 3)
    events = listed(EVENTS, inside)
    use = listed(USE, inside)
    give = listed(GIVE, inside)
    f32, bf16 = jnp.float32, jnp.bfloat16

    def target(cz, cx, cc):
        return {"row": (cz * xs + cx) * 2 + cc}

    def piece_at(code):
        near = code // 4
        cz = jnp.where(low, near, 3 - near)
        cx = jnp.where((code // 2) % 2 == 1, 1 - x, x)
        return cz, cx, cz * xs + cx, code % 2

    def weights(step, fn):
        _, _, chip, n = piece_at(entry(use, step))
        slot = step % 3
        cols = pl.ds(pl.multiple_of(chip * width, 128), width)

        @pl.when(n == 0)
        def _():
            fn(pltpu.make_async_copy(wg_ref.at[:, cols], wgu.at[chip, :hidden], wsem.at[slot, 0]))
            fn(pltpu.make_async_copy(wu_ref.at[:, cols], wgu.at[chip, hidden:], wsem.at[slot, 1]))

        @pl.when(n == 1)
        def _():
            fn(pltpu.make_async_copy(wd_ref.at[:, cols], wdn.at[slot], wsem.at[slot, 0]))

    def passing(cz, cx, chip, n, src, fn):
        two = ((cz == 0) | (cz == zs - 1)) & (n == 1)
        column = cx == x
        along = column | two

        def copy(tz, tx, tc, way):
            return lambda: fn(
                pltpu.make_async_remote_copy(
                    src_ref=src,
                    dst_ref=held.at[chip, n, core],
                    send_sem=send_sem.at[way, chip, n],
                    recv_sem=recv_sem.at[chip, n, core],
                    device_id=target(tz, tx, tc),
                    device_id_type=MESH,
                )
            )

        pl.when(along & (cz <= z) & (z < zs - 1))(copy(z + 1, x, core, 0))
        pl.when(along & (cz >= z) & (z > 0))(copy(z - 1, x, core, 1))
        pl.when(column & (jnp.logical_not(two) | (cz == z)))(copy(z, 1 - x, core, 2))
        copy(z, x, 1 - core, 3)()

    def arrive(chip, n, which):
        block = held.at[chip, n, which]
        pltpu.make_async_copy(block, block, recv_sem.at[chip, n, which]).wait()

    own = [
        pltpu.make_async_copy(ref, held.at[mine, n, core], own_sem.at[n])
        for n, ref in enumerate((x_ref, dy_ref))
    ]
    for c in own:
        c.start()
    greet(z, x, core, zs, xs)
    for n, ref in enumerate((x_ref, dy_ref)):
        passing(z, x, mine, n, ref, lambda c: c.start())
    weights(0, lambda c: c.start())
    weights(1, lambda c: c.start())
    acc[...] = jnp.zeros_like(acc)
    for c in own:
        c.wait()

    part_rows = 128 if hidden % 128 == 0 else hidden

    def gather(step, carry):
        event = entry(events, step)

        @pl.when(event < 16)
        def _():
            cz, cx, chip, n = piece_at(event)
            arrive(chip, n, core)
            passing(cz, cx, chip, n, held.at[chip, n, core], lambda c: c.start())

        @pl.when((event >= 16) & (event < 32))
        def _():
            count = event - 16
            cz, cx, chip, n = piece_at(entry(use, count))
            pl.when(count + 2 < 16)(lambda: weights(count + 2, lambda c: c.start()))
            arrive(chip, n, 1 - core)
            pltpu.make_async_copy(held.at[chip, n], all_ref.at[n, chip], all_sem.at[n, chip]).start()
            weights(count, lambda c: c.wait())

            @pl.when(n == 0)
            def _():
                block = held[chip, 0].reshape(width, tokens)
                acc[0] += jnp.dot(wgu[chip, :hidden], block, preferred_element_type=f32)
                acc[1] += jnp.dot(wgu[chip, hidden:], block, preferred_element_type=f32)

            @pl.when(n == 1)
            def _():
                block = held[chip, 1].reshape(width, tokens)
                acc[2] += jnp.dot(wdn[count % 3], block, preferred_element_type=f32)

        @pl.when(event == 32)
        def _():
            for start in range(0, hidden, part_rows):
                at = slice(start, start + part_rows)
                gate_pre, up_pre = acc[0, at], acc[1, at]
                sig = jax.nn.sigmoid(gate_pre)
                act = gate_pre * sig
                hact[at] = (act * up_pre).astype(bf16)
                acc[0, at] = up_pre * sig * (1.0 + gate_pre * (1.0 - sig))
                acc[1, at] = act

        return carry

    lax.fori_loop(0, len(EVENTS[0]), gather, 0)

    for start in range(0, hidden, part_rows):
        at = slice(start, start + part_rows)
        hidden_grad = acc[2, at]
        grad_gate_pre = (hidden_grad * acc[0, at]).astype(bf16)
        grad_up_pre = (hidden_grad * acc[1, at]).astype(bf16)
        ggp[at] = grad_gate_pre
        turned[:, at] = grad_gate_pre.T
        gup[at] = grad_up_pre
        turned[:, hidden + start : hidden + start + part_rows] = grad_up_pre.T
    small = [
        pltpu.make_async_copy(src, dst, small_sem.at[n])
        for n, (src, dst) in enumerate(((hact, hact_ref), (ggp, pre_ref.at[0]), (gup, pre_ref.at[1])))
    ]
    for c in small:
        c.start()

    def to_core(chip, h):
        at = pl.ds(pl.multiple_of(h * tokens, tokens), tokens)
        return pltpu.make_async_remote_copy(
            src_ref=outb.at[chip, at],
            dst_ref=core_in.at[chip, at],
            send_sem=core_send.at[chip, h],
            recv_sem=core_recv.at[chip, h],
            device_id=target(z, x, 1 - core),
            device_id_type=MESH,
        )

    def onward(cz, cx, chip, h, fn):
        two = ((cz == 0) | (cz == zs - 1)) & (h == 1)
        along = (cx == x) | two
        at = pl.ds(pl.multiple_of(h * tokens, tokens), tokens)

        def line(tz, tx, dst, sem):
            return lambda: fn(
                pltpu.make_async_remote_copy(
                    src_ref=outb.at[chip, at],
                    dst_ref=dst,
                    send_sem=line_send.at[chip, h],
                    recv_sem=sem,
                    device_id=target(tz, tx, core),
                    device_id_type=MESH,
                )
            )

        pl.when(along & (cz > z))(line(z + 1, x, z_in.at[0, chip, at], z_recv.at[0, chip, h]))
        pl.when(along & (cz < z))(line(z - 1, x, z_in.at[1, chip, at], z_recv.at[1, chip, h]))
        pl.when((cx != x) & (jnp.logical_not(two) | (cz == z)))(
            line(z, 1 - x, x_in.at[cz, at], x_recv.at[cz, h])
        )

    def block_at(code):
        near = code // 2
        cz = jnp.where(low, near, 3 - near)
        cx = jnp.where(code % 2 == 1, 1 - x, x)
        return cz, cx, cz * xs + cx

    def scatter(step, carry):
        code = entry(give, step)

        @pl.when(code < 8)
        def _():
            _, _, chip = block_at(code)

            def product(which):
                cols = pl.ds(pl.multiple_of(which * rows, 128), rows)
                return jnp.dot(turned[...], wgu[chip, :, cols], preferred_element_type=f32)

            total = product(1 - core)
            for h in range(2):
                at = slice(h * tokens, (h + 1) * tokens)
                outb[chip, at] = total[:, h * half : (h + 1) * half].astype(bf16)
                to_core(chip, h).start()
            total = product(core)
            for h in range(2):
                at = slice(h * tokens, (h + 1) * tokens)
                part[chip, at] = total[:, h * half : (h + 1) * half]

        @pl.when(code >= 8)
        def _():
            h = code % 2
            cz, cx, chip = block_at((code - 8) // 2)
            two = ((cz == 0) | (cz == zs - 1)) & (h == 1)
            along = (cx == x) | two
            at = pl.ds(pl.multiple_of(h * tokens, tokens), tokens)
            to_core(chip, h).wait()
            part[chip, at] += core_in[chip, at].astype(f32)

            def gain(block, sem):
                def run():
                    pltpu.make_async_copy(block, block, sem).wait()
                    part[chip, at] += block[...].astype(f32)

                return run

            pl.when((cx == x) & (jnp.logical_not(two) | (cz == z)))(
                gain(x_in.at[cz, at], x_recv.at[cz, h])
            )
            pl.when(along & (cz >= z) & (z > 0))(gain(z_in.at[0, chip, at], z_recv.at[0, chip, h]))
            pl.when(along & (cz <= z) & (z < zs - 1))(
                gain(z_in.at[1, chip, at], z_recv.at[1, chip, h])
            )
            outb[chip, at] = part[chip, at].astype(bf16)
            onward(cz, cx, chip, h, lambda c: c.start())

        @pl.when(step >= len(GIVE[0]) - 16)
        def _():
            cz, cx, chip, n = piece_at(step - (len(GIVE[0]) - 16))
            passing(cz, cx, chip, n, held.at[chip, n, core], lambda c: c.wait_send())
            pltpu.make_async_copy(held.at[chip, n], all_ref.at[n, chip], all_sem.at[n, chip]).wait()

        return carry

    lax.fori_loop(0, len(GIVE[0]), scatter, 0)
    for h in range(2):
        grad_ref[h * half : (h + 1) * half] = outb[mine, h * tokens : (h + 1) * tokens].T

    for c in small:
        c.wait()

    def drain(step, carry):
        cz, cx, chip, n = piece_at(step)
        onward(cz, cx, chip, n, lambda c: c.wait_send())
        return carry

    lax.fori_loop(0, 16, drain, 0)


def weight_grads_kernel(
    hact_ref, pre_ref, x_ref, dy_ref, gate_ref, up_ref, down_ref
):
    bf16 = jnp.bfloat16
    hidden = gate_ref.shape[0]
    both = over_tokens(pre_ref[...], x_ref[0]).astype(bf16)
    gate_ref[...] = both[:hidden]
    up_ref[...] = both[hidden:]
    down_ref[...] = over_tokens(hact_ref[...], dy_ref[0]).astype(bf16)


def on_grid(layer_input, output_grad, gate_weight, up_weight, down_weight):
    chips = 8
    rows, tokens = layer_input.shape
    hidden, features = gate_weight.shape
    width = 2 * rows
    half = rows // 2
    bf16, f32 = jnp.bfloat16, jnp.float32
    anywhere = pl.BlockSpec(memory_space=pl.ANY)
    vmem = pl.BlockSpec(memory_space=pltpu.VMEM)
    DMA = pltpu.SemaphoreType.DMA
    VMEM = pltpu.VMEM
    small = jax.ShapeDtypeStruct((hidden, tokens), bf16)
    grad, hact, pre, gathered = pl.pallas_call(
        grid_kernel,
        out_shape=(
            jax.ShapeDtypeStruct((rows, tokens), bf16),
            small, jax.ShapeDtypeStruct((2, hidden, tokens), bf16),
            jax.ShapeDtypeStruct((2, chips, 2, rows, tokens), bf16),
        ),
        in_specs=[anywhere] * 5,
        out_specs=(vmem, anywhere, anywhere, anywhere),
        scratch_shapes=[
            VMEM((chips, 2, 2, rows, tokens), bf16),
            VMEM((chips, 2 * hidden, width), bf16),
            VMEM((3, hidden, width), bf16),
            VMEM((3, hidden, tokens), f32),
            VMEM((hidden, tokens), bf16),
            VMEM((hidden, tokens), bf16),
            VMEM((hidden, tokens), bf16),
            VMEM((tokens, 2 * hidden), bf16),
            VMEM((chips, 2 * tokens, half), f32),
            VMEM((chips, 2 * tokens, half), bf16),
            VMEM((chips, 2 * tokens, half), bf16),
            VMEM((4, 2 * tokens, half), bf16),
            VMEM((2, chips, 2 * tokens, half), bf16),
            DMA((2,)),
            DMA((3, 2)),
            DMA((4, chips, 2)),
            DMA((chips, 2, 2)),
            DMA((2, chips)),
            DMA((3,)),
            DMA((chips, 2)),
            DMA((chips, 2)),
            DMA((chips, 2)),
            DMA((4, 2)),
            DMA((2, chips, 2)),
        ],
        compiler_params=pltpu.CompilerParams(
            collective_id=0, has_side_effects=True, vmem_limit_bytes=GRID_VMEM
        ),
        name="gather_scatter",
    )(layer_input, output_grad, gate_weight, up_weight, down_weight)
    gathered = gathered.reshape(2, features, tokens)
    block = 1024

    def fixed(shape):
        return pl.BlockSpec(shape, lambda j: (0, 0))

    grads = jax.ShapeDtypeStruct((hidden, features), bf16)
    columns = pl.BlockSpec((hidden, block), lambda j: (0, j))
    gate_grad, up_grad, down_grad = pl.pallas_call(
        weight_grads_kernel,
        grid=(features // block,),
        out_shape=(grads, grads, grads),
        in_specs=[
            fixed((hidden, tokens)),
            fixed((2 * hidden, tokens)),
            pl.BlockSpec((1, block, tokens), lambda j: (0, j, 0)),
            pl.BlockSpec((1, block, tokens), lambda j: (1, j, 0)),
        ],
        out_specs=(columns, columns, columns),
        compiler_params=pltpu.CompilerParams(vmem_limit_bytes=VMEM_LIMIT),
        name="weight_grads",
    )(hact, pre.reshape(2 * hidden, tokens), gathered, gathered)
    return (grad, gate_grad, up_grad, down_grad)


def solution(mesh):
    row = mesh.shape["row"]
    xs = 2 if row <= 16 else 4
    zs = row // (2 * xs)
    return jax.shard_map(
        on_grid if (zs, xs) == (4, 2) else functools.partial(on_device, zs, xs),
        mesh=mesh,
        in_specs=(
            P("row", "groups"),
            P("row", "groups"),
            P(("groups", "row"), None),
            P(("groups", "row"), None),
            P(("groups", "row"), None),
        ),
        out_specs=(
            P("row", "groups"),
            P(("groups", "row"), None),
            P(("groups", "row"), None),
            P(("groups", "row"), None),
        ),
        check_vma=False,
    )
```

```python
import functools

import jax
import jax.numpy as jnp
from jax import lax
from jax.experimental import pallas as pl
from jax.experimental.pallas import tpu as pltpu
from jax.sharding import PartitionSpec as P

MESH = pl.DeviceIdType.MESH
VMEM_LIMIT = 64 * 1000 * 1000
GRID_VMEM = 64 * 1024 * 1024


def over_tokens(first_mat, second_mat):
    return lax.dot_general(
        first_mat, second_mat, (((1,), (1,)), ((), ())), preferred_element_type=jnp.float32
    )


def nearest(rank, here, extent):
    low = jnp.minimum(here, extent - 1 - here)
    half = (rank + 1) // 2
    both = jnp.where(rank % 2 == 1, here + half, here - half)
    one = jnp.where(here < extent - 1 - here, rank, extent - 1 - rank)
    return jnp.where(rank <= 2 * low, both, one)


def place(zs, xs):
    me = lax.axis_index("row")
    core = me % 2
    x = (me // 2) % xs
    z = me // (2 * xs)
    return z, x, core


def chip_at(step, z, x, zs, xs):
    if xs == 2:
        inner = (step > 0) & (step < 2 * zs - 1)
        beside = jnp.where(inner, (step + 1) % 2, jnp.minimum(step, 1))
        rank = jnp.where(inner, (step + 1) // 2 - beside, step // 2)
    else:
        rank, beside = step // xs, step % xs
    cz = nearest(rank, z, zs)
    cx = nearest(beside, x, xs)
    return cz, cx, cz * xs + cx


def greet(z, x, core, zs, xs):
    barrier = pltpu.get_barrier_semaphore()

    def hail(cz, cx, cc):
        pl.semaphore_signal(
            barrier, inc=1, device_id={"row": (cz * xs + cx) * 2 + cc}, device_id_type=MESH
        )

    hail(z, x, 1 - core)
    pl.when(z > 0)(lambda: hail(z - 1, x, core))
    pl.when(z < zs - 1)(lambda: hail(z + 1, x, core))
    pl.when(x > 0)(lambda: hail(z, x - 1, core))
    pl.when(x < xs - 1)(lambda: hail(z, x + 1, core))
    count = 1 + jnp.minimum(z, 1) + jnp.minimum(zs - 1 - z, 1)
    count = count + jnp.minimum(x, 1) + jnp.minimum(xs - 1 - x, 1)
    pl.semaphore_wait(barrier, count)


def forward_kernel(
    zs, xs, x_ref, dy_ref, wg_ref, wu_ref, wd_ref,
    hact_ref, ggp_ref, gup_ref, ggp_t_ref, gup_t_ref, xg_ref, dyg_ref,
    held, wbuf, acc, send_sem, recv_sem, wsem, own_sem, out_sem,
):
    z, x, core = place(zs, xs)
    mine = z * xs + x
    chips = zs * xs
    rows, hidden = held.shape[3], acc.shape[1]
    width = 2 * rows
    tokens = held.shape[4]

    def weights(step, fn):
        _, _, chip = chip_at(step, z, x, zs, xs)
        cols = pl.ds(pl.multiple_of(chip * width, 128), width)
        slot = step % 2
        for n, ref in enumerate((wg_ref, wu_ref, wd_ref)):
            fn(pltpu.make_async_copy(ref.at[:, cols], wbuf.at[slot, n], wsem.at[slot, n]))

    weights(0, lambda c: c.start())
    own = [
        pltpu.make_async_copy(ref, held.at[mine, n, core], own_sem.at[n])
        for n, ref in enumerate((x_ref, dy_ref))
    ]
    for c in own:
        c.start()
    greet(z, x, core, zs, xs)
    for c in own:
        c.wait()

    def passing(step, fn):
        cz, cx, chip = chip_at(step, z, x, zs, xs)
        block = held.at[chip, :, core]

        def copy(tz, tx, tc, n):
            return lambda: fn(
                pltpu.make_async_remote_copy(
                    src_ref=block,
                    dst_ref=block,
                    send_sem=send_sem.at[n, chip],
                    recv_sem=recv_sem.at[chip, core],
                    device_id={"row": (tz * xs + tx) * 2 + tc},
                    device_id_type=MESH,
                )
            )

        pl.when((cx == x) & (cz <= z) & (z < zs - 1))(copy(z + 1, x, core, 0))
        pl.when((cx == x) & (cz >= z) & (z > 0))(copy(z - 1, x, core, 1))
        pl.when((cx <= x) & (x < xs - 1))(copy(z, x + 1, core, 2))
        pl.when((cx >= x) & (x > 0))(copy(z, x - 1, core, 3))
        copy(z, x, 1 - core, 4)()

    def arrive(step, which):
        _, _, chip = chip_at(step, z, x, zs, xs)
        block = held.at[chip, :, which]
        pltpu.make_async_copy(block, block, recv_sem.at[chip, which]).wait()

    passing(0, lambda c: c.start())
    acc[...] = jnp.zeros_like(acc)

    def body(step, carry):
        @pl.when(step + 1 < chips)
        def _():
            weights(step + 1, lambda c: c.start())
            arrive(step + 1, core)
            passing(step + 1, lambda c: c.start())

        arrive(step, 1 - core)
        weights(step, lambda c: c.wait())
        _, _, chip = chip_at(step, z, x, zs, xs)
        for n, ref in enumerate((xg_ref, dyg_ref)):
            pltpu.make_async_copy(held.at[chip, n], ref.at[chip], out_sem.at[n, chip]).start()
        slot = step % 2
        x_block = held[chip, 0].reshape(width, tokens)
        acc[0] += jnp.dot(wbuf[slot, 0], x_block, preferred_element_type=jnp.float32)
        acc[1] += jnp.dot(wbuf[slot, 1], x_block, preferred_element_type=jnp.float32)
        dy_block = held[chip, 1].reshape(width, tokens)
        acc[2] += jnp.dot(wbuf[slot, 2], dy_block, preferred_element_type=jnp.float32)
        return carry

    lax.fori_loop(0, chips, body, 0)

    part = 128 if hidden % 128 == 0 else hidden
    for start in range(0, hidden, part):
        at = slice(start, start + part)
        gate_pre, up_pre, hidden_grad = acc[0, at], acc[1, at], acc[2, at]
        sig = jax.nn.sigmoid(gate_pre)
        act = gate_pre * sig
        hact_ref[at] = (act * up_pre).astype(jnp.bfloat16)
        grad_gate_pre = hidden_grad * up_pre * sig * (1.0 + gate_pre * (1.0 - sig))
        ggp_ref[at] = grad_gate_pre.astype(jnp.bfloat16)
        ggp_t_ref[:, at] = grad_gate_pre.T.astype(jnp.bfloat16)
        grad_up_pre = hidden_grad * act
        gup_ref[at] = grad_up_pre.astype(jnp.bfloat16)
        gup_t_ref[:, at] = grad_up_pre.T.astype(jnp.bfloat16)

    def drain(step, carry):
        _, _, chip = chip_at(step, z, x, zs, xs)
        passing(step, lambda c: c.wait_send())
        for n, ref in enumerate((xg_ref, dyg_ref)):
            pltpu.make_async_copy(held.at[chip, n], ref.at[chip], out_sem.at[n, chip]).wait()
        return carry

    lax.fori_loop(0, chips, drain, 0)


def scatter_kernel(
    zs, xs, ggp_ref, gup_ref, wg_ref, wu_ref, out_ref,
    wbuf, part, core_out, core_in, line_out, x_in, z_in,
    wsem, core_send, core_recv, line_send, x_recv, z_recv,
):
    z, x, core = place(zs, xs)
    chips = zs * xs
    rows, tokens = out_ref.shape
    width = 2 * rows

    def chip_of(step):
        return chip_at(chips - 1 - step, z, x, zs, xs)

    def weights(step, fn):
        _, _, chip = chip_of(step)
        cols = pl.ds(pl.multiple_of(chip * width, 128), width)
        slot = step % 2
        for n, ref in enumerate((wg_ref, wu_ref)):
            fn(pltpu.make_async_copy(ref.at[:, cols], wbuf.at[slot, n], wsem.at[slot, n]))

    def to_core(chip):
        return pltpu.make_async_remote_copy(
            src_ref=core_out.at[chip],
            dst_ref=core_in.at[chip],
            send_sem=core_send.at[chip],
            recv_sem=core_recv.at[chip],
            device_id={"row": (z * xs + x) * 2 + 1 - core},
            device_id_type=MESH,
        )

    def line(chip, tz, tx, buf, sems, side):
        return pltpu.make_async_remote_copy(
            src_ref=line_out.at[chip],
            dst_ref=buf.at[side, chip],
            send_sem=line_send.at[chip],
            recv_sem=sems.at[side, chip],
            device_id={"row": (tz * xs + tx) * 2 + core},
            device_id_type=MESH,
        )

    def onward(cz, cx, chip, fn):
        pl.when(cx > x)(lambda: fn(line(chip, z, x + 1, x_in, x_recv, 0)))
        pl.when(cx < x)(lambda: fn(line(chip, z, x - 1, x_in, x_recv, 1)))
        pl.when((cx == x) & (cz > z))(lambda: fn(line(chip, z + 1, x, z_in, z_recv, 0)))
        pl.when((cx == x) & (cz < z))(lambda: fn(line(chip, z - 1, x, z_in, z_recv, 1)))

    weights(0, lambda c: c.start())
    greet(z, x, core, zs, xs)

    def make(step):
        slot = step % 2
        _, _, chip = chip_of(step)

        @pl.when(step + 1 < chips)
        def _():
            weights(step + 1, lambda c: c.start())

        weights(step, lambda c: c.wait())
        total = jnp.dot(ggp_ref[...], wbuf[slot, 0], preferred_element_type=jnp.float32)
        total += jnp.dot(gup_ref[...], wbuf[slot, 1], preferred_element_type=jnp.float32)
        part[slot] = total.T.reshape(2, rows, tokens)
        core_out[chip] = part[slot, 1 - core].astype(jnp.bfloat16)
        to_core(chip).start()

    def add(step):
        slot = step % 2
        cz, cx, chip = chip_of(step)
        to_core(chip).wait_recv()
        part[slot, core] += core_in[chip].astype(jnp.float32)

        def take(buf, sems, side):
            def run():
                block = buf.at[side, chip]
                pltpu.make_async_copy(block, block, sems.at[side, chip]).wait()
                part[slot, core] += buf[side, chip].astype(jnp.float32)

            return run

        pl.when((cx >= x) & (x > 0))(take(x_in, x_recv, 0))
        pl.when((cx <= x) & (x < xs - 1))(take(x_in, x_recv, 1))
        pl.when((cx == x) & (cz >= z) & (z > 0))(take(z_in, z_recv, 0))
        pl.when((cx == x) & (cz <= z) & (z < zs - 1))(take(z_in, z_recv, 1))
        line_out[chip] = part[slot, core].astype(jnp.bfloat16)
        onward(cz, cx, chip, lambda c: c.start())

    make(0)

    def body(step, carry):
        make(step)
        add(step - 1)
        return carry

    lax.fori_loop(1, chips, body, 0)
    add(chips - 1)
    out_ref[...] = line_out[z * xs + x]

    def drain(step, carry):
        cz, cx, chip = chip_of(step)
        to_core(chip).wait_send()
        onward(cz, cx, chip, lambda c: c.wait_send())
        return carry

    lax.fori_loop(0, chips, drain, 0)


def on_device(zs, xs, layer_input, output_grad, gate_weight, up_weight, down_weight):
    chips = zs * xs
    rows, tokens = layer_input.shape
    hidden, features = gate_weight.shape
    width = 2 * rows
    bf16, f32 = jnp.bfloat16, jnp.float32
    anywhere = pl.BlockSpec(memory_space=pl.ANY)
    vmem = pl.BlockSpec(memory_space=pltpu.VMEM)
    DMA = pltpu.SemaphoreType.DMA
    small = jax.ShapeDtypeStruct((hidden, tokens), bf16)
    turned = jax.ShapeDtypeStruct((tokens, hidden), bf16)
    whole = jax.ShapeDtypeStruct((chips, 2, rows, tokens), bf16)
    hidden_act, ggp, gup, ggp_t, gup_t, xg, dyg = pl.pallas_call(
        functools.partial(forward_kernel, zs, xs),
        out_shape=(small, small, small, turned, turned, whole, whole),
        in_specs=[anywhere] * 5,
        out_specs=(vmem, vmem, vmem, vmem, vmem, anywhere, anywhere),
        scratch_shapes=[
            pltpu.VMEM((chips, 2, 2, rows, tokens), bf16),
            pltpu.VMEM((2, 3, hidden, width), bf16),
            pltpu.VMEM((3, hidden, tokens), f32),
            DMA((5, chips)),
            DMA((chips, 2)),
            DMA((2, 3)),
            DMA((2,)),
            DMA((2, chips)),
        ],
        compiler_params=pltpu.CompilerParams(
            collective_id=0, has_side_effects=True, vmem_limit_bytes=VMEM_LIMIT
        ),
        name="gather_forward",
    )(layer_input, output_grad, gate_weight, up_weight, down_weight)
    input_grad = pl.pallas_call(
        functools.partial(scatter_kernel, zs, xs),
        out_shape=jax.ShapeDtypeStruct((rows, tokens), bf16),
        in_specs=[vmem, vmem, anywhere, anywhere],
        out_specs=vmem,
        scratch_shapes=[
            pltpu.VMEM((2, 2, hidden, width), bf16),
            pltpu.VMEM((2, 2, rows, tokens), f32),
            pltpu.VMEM((chips, rows, tokens), bf16),
            pltpu.VMEM((chips, rows, tokens), bf16),
            pltpu.VMEM((chips, rows, tokens), bf16),
            pltpu.VMEM((2, chips, rows, tokens), bf16),
            pltpu.VMEM((2, chips, rows, tokens), bf16),
            DMA((2, 2)),
            DMA((chips,)),
            DMA((chips,)),
            DMA((chips,)),
            DMA((2, chips)),
            DMA((2, chips)),
        ],
        compiler_params=pltpu.CompilerParams(
            collective_id=1, has_side_effects=True, vmem_limit_bytes=VMEM_LIMIT
        ),
        name="scatter_input_grad",
    )(ggp_t, gup_t, gate_weight, up_weight)
    block_in = xg.reshape(features, tokens)
    block_dy = dyg.reshape(features, tokens)
    down_grad = over_tokens(hidden_act, block_dy).astype(bf16)
    gate_grad = over_tokens(ggp, block_in).astype(bf16)
    up_grad = over_tokens(gup, block_in).astype(bf16)
    return (input_grad, gate_grad, up_grad, down_grad)


EVENTS = (
    (16, 17, 5, 4, 18, 19, 8, 3, 20, 21, 12, 6, 9, 2, 22, 23, 24, 25, 14, 10, 13, 7, 26, 27, 32, 28, 15, 29,
     11, 30, 31),
    (16, 17, 0, 8, 6, 18, 19, 20, 7, 1, 9, 21, 22, 23, 12, 24, 10, 2, 25, 3, 13, 26, 27, 28, 15, 11, 29, 14,
     30, 31, 32),
)
USE = (
    (0, 1, 5, 4, 8, 3, 12, 2, 6, 9, 14, 10, 7, 13, 15, 11),
    (4, 5, 0, 6, 8, 7, 1, 9, 12, 10, 2, 3, 13, 15, 11, 14),
)
GIVE = (
    (7, 5, 22, 23, 6, 18, 19, 4, 21, 0, 20, 3, 1, 14, 16, 15, 2, 10, 17, 12, 11, 13, 8, 9),
    (1, 7, 10, 6, 22, 5, 4, 18, 19, 3, 0, 14, 15, 2, 23, 21, 11, 20, 9, 16, 8, 17, 12, 13),
)


def listed(rows, inside):
    return [jnp.where(inside, b, a) for a, b in zip(*rows)]


def entry(values, step):
    found = values[0]
    for n, value in enumerate(values[1:], 1):
        found = jnp.where(step == n, value, found)
    return found


def grid_kernel(
    x_ref, dy_ref, wg_ref, wu_ref, wd_ref,
    grad_ref, hact_ref, pre_ref, all_ref,
    held, wgu, wdn, acc, hact, ggp, gup, turned, part, outb, core_in, x_in, z_in,
    own_sem, wsem, send_sem, recv_sem, all_sem, small_sem,
    core_send, core_recv, line_send, x_recv, z_recv,
):
    zs, xs = 4, 2
    z, x, core = place(zs, xs)
    mine = z * xs + x
    rows, hidden, tokens = held.shape[3], acc.shape[1], acc.shape[2]
    width = 2 * rows
    half = rows // 2
    low = z < 2
    inside = (z > 0) & (z < 3)
    events = listed(EVENTS, inside)
    use = listed(USE, inside)
    give = listed(GIVE, inside)
    f32, bf16 = jnp.float32, jnp.bfloat16

    def target(cz, cx, cc):
        return {"row": (cz * xs + cx) * 2 + cc}

    def piece_at(code):
        near = code // 4
        cz = jnp.where(low, near, 3 - near)
        cx = jnp.where((code // 2) % 2 == 1, 1 - x, x)
        return cz, cx, cz * xs + cx, code % 2

    def weights(step, fn):
        _, _, chip, n = piece_at(entry(use, step))
        slot = step % 3
        cols = pl.ds(pl.multiple_of(chip * width, 128), width)

        @pl.when(n == 0)
        def _():
            fn(pltpu.make_async_copy(wg_ref.at[:, cols], wgu.at[chip, :hidden], wsem.at[slot, 0]))
            fn(pltpu.make_async_copy(wu_ref.at[:, cols], wgu.at[chip, hidden:], wsem.at[slot, 1]))

        @pl.when(n == 1)
        def _():
            fn(pltpu.make_async_copy(wd_ref.at[:, cols], wdn.at[slot], wsem.at[slot, 0]))

    def passing(cz, cx, chip, n, src, fn):
        two = ((cz == 0) | (cz == zs - 1)) & (n == 1)
        column = cx == x
        along = column | two

        def copy(tz, tx, tc, way):
            return lambda: fn(
                pltpu.make_async_remote_copy(
                    src_ref=src,
                    dst_ref=held.at[chip, n, core],
                    send_sem=send_sem.at[way, chip, n],
                    recv_sem=recv_sem.at[chip, n, core],
                    device_id=target(tz, tx, tc),
                    device_id_type=MESH,
                )
            )

        pl.when(along & (cz <= z) & (z < zs - 1))(copy(z + 1, x, core, 0))
        pl.when(along & (cz >= z) & (z > 0))(copy(z - 1, x, core, 1))
        pl.when(column & (jnp.logical_not(two) | (cz == z)))(copy(z, 1 - x, core, 2))
        copy(z, x, 1 - core, 3)()

    def arrive(chip, n, which):
        block = held.at[chip, n, which]
        pltpu.make_async_copy(block, block, recv_sem.at[chip, n, which]).wait()

    own = [
        pltpu.make_async_copy(ref, held.at[mine, n, core], own_sem.at[n])
        for n, ref in enumerate((x_ref, dy_ref))
    ]
    for c in own:
        c.start()
    weights(0, lambda c: c.start())
    weights(1, lambda c: c.start())
    acc[...] = jnp.zeros_like(acc)
    greet(z, x, core, zs, xs)
    for n, ref in enumerate((x_ref, dy_ref)):
        passing(z, x, mine, n, ref, lambda c: c.start())
    for c in own:
        c.wait()

    part_rows = 128 if hidden % 128 == 0 else hidden

    def gather(step, carry):
        event = entry(events, step)

        @pl.when(event < 16)
        def _():
            cz, cx, chip, n = piece_at(event)
            arrive(chip, n, core)
            passing(cz, cx, chip, n, held.at[chip, n, core], lambda c: c.start())

        @pl.when((event >= 16) & (event < 32))
        def _():
            count = event - 16
            cz, cx, chip, n = piece_at(entry(use, count))
            pl.when(count + 2 < 16)(lambda: weights(count + 2, lambda c: c.start()))
            arrive(chip, n, 1 - core)
            pltpu.make_async_copy(held.at[chip, n], all_ref.at[n, chip], all_sem.at[n, chip]).start()
            weights(count, lambda c: c.wait())

            @pl.when(n == 0)
            def _():
                block = held[chip, 0].reshape(width, tokens)
                acc[0] += jnp.dot(wgu[chip, :hidden], block, preferred_element_type=f32)
                acc[1] += jnp.dot(wgu[chip, hidden:], block, preferred_element_type=f32)

            @pl.when(n == 1)
            def _():
                block = held[chip, 1].reshape(width, tokens)
                acc[2] += jnp.dot(wdn[count % 3], block, preferred_element_type=f32)

        @pl.when(event == 32)
        def _():
            for start in range(0, hidden, part_rows):
                at = slice(start, start + part_rows)
                gate_pre, up_pre = acc[0, at], acc[1, at]
                sig = jax.nn.sigmoid(gate_pre)
                act = gate_pre * sig
                hact[at] = (act * up_pre).astype(bf16)
                acc[0, at] = up_pre * sig * (1.0 + gate_pre * (1.0 - sig))
                acc[1, at] = act

        return carry

    lax.fori_loop(0, len(EVENTS[0]), gather, 0)

    for start in range(0, hidden, part_rows):
        at = slice(start, start + part_rows)
        hidden_grad = acc[2, at]
        grad_gate_pre = (hidden_grad * acc[0, at]).astype(bf16)
        grad_up_pre = (hidden_grad * acc[1, at]).astype(bf16)
        ggp[at] = grad_gate_pre
        turned[:, at] = grad_gate_pre.T
        gup[at] = grad_up_pre
        turned[:, hidden + start : hidden + start + part_rows] = grad_up_pre.T
    small = [
        pltpu.make_async_copy(src, dst, small_sem.at[n])
        for n, (src, dst) in enumerate(((hact, hact_ref), (ggp, pre_ref.at[0]), (gup, pre_ref.at[1])))
    ]
    for c in small:
        c.start()

    def to_core(chip, h):
        at = pl.ds(pl.multiple_of(h * tokens, tokens), tokens)
        return pltpu.make_async_remote_copy(
            src_ref=outb.at[chip, at],
            dst_ref=core_in.at[chip, at],
            send_sem=core_send.at[chip, h],
            recv_sem=core_recv.at[chip, h],
            device_id=target(z, x, 1 - core),
            device_id_type=MESH,
        )

    def onward(cz, cx, chip, h, fn):
        two = ((cz == 0) | (cz == zs - 1)) & (h == 1)
        along = (cx == x) | two
        at = pl.ds(pl.multiple_of(h * tokens, tokens), tokens)

        def line(tz, tx, dst, sem):
            return lambda: fn(
                pltpu.make_async_remote_copy(
                    src_ref=outb.at[chip, at],
                    dst_ref=dst,
                    send_sem=line_send.at[chip, h],
                    recv_sem=sem,
                    device_id=target(tz, tx, core),
                    device_id_type=MESH,
                )
            )

        pl.when(along & (cz > z))(line(z + 1, x, z_in.at[0, chip, at], z_recv.at[0, chip, h]))
        pl.when(along & (cz < z))(line(z - 1, x, z_in.at[1, chip, at], z_recv.at[1, chip, h]))
        pl.when((cx != x) & (jnp.logical_not(two) | (cz == z)))(
            line(z, 1 - x, x_in.at[cz, at], x_recv.at[cz, h])
        )

    def block_at(code):
        near = code // 2
        cz = jnp.where(low, near, 3 - near)
        cx = jnp.where(code % 2 == 1, 1 - x, x)
        return cz, cx, cz * xs + cx

    def scatter(step, carry):
        code = entry(give, step)

        @pl.when(code < 8)
        def _():
            _, _, chip = block_at(code)

            def product(which):
                cols = pl.ds(pl.multiple_of(which * rows, 128), rows)
                return jnp.dot(turned[...], wgu[chip, :, cols], preferred_element_type=f32)

            total = product(1 - core)
            for h in range(2):
                at = slice(h * tokens, (h + 1) * tokens)
                outb[chip, at] = total[:, h * half : (h + 1) * half].astype(bf16)
                to_core(chip, h).start()
            total = product(core)
            for h in range(2):
                at = slice(h * tokens, (h + 1) * tokens)
                part[chip, at] = total[:, h * half : (h + 1) * half]

        @pl.when(code >= 8)
        def _():
            h = code % 2
            cz, cx, chip = block_at((code - 8) // 2)
            two = ((cz == 0) | (cz == zs - 1)) & (h == 1)
            along = (cx == x) | two
            at = pl.ds(pl.multiple_of(h * tokens, tokens), tokens)
            to_core(chip, h).wait()
            part[chip, at] += core_in[chip, at].astype(f32)

            def gain(block, sem):
                def run():
                    pltpu.make_async_copy(block, block, sem).wait()
                    part[chip, at] += block[...].astype(f32)

                return run

            pl.when((cx == x) & (jnp.logical_not(two) | (cz == z)))(
                gain(x_in.at[cz, at], x_recv.at[cz, h])
            )
            pl.when(along & (cz >= z) & (z > 0))(gain(z_in.at[0, chip, at], z_recv.at[0, chip, h]))
            pl.when(along & (cz <= z) & (z < zs - 1))(
                gain(z_in.at[1, chip, at], z_recv.at[1, chip, h])
            )
            outb[chip, at] = part[chip, at].astype(bf16)
            onward(cz, cx, chip, h, lambda c: c.start())

        @pl.when(step >= len(GIVE[0]) - 16)
        def _():
            cz, cx, chip, n = piece_at(step - (len(GIVE[0]) - 16))
            passing(cz, cx, chip, n, held.at[chip, n, core], lambda c: c.wait_send())
            pltpu.make_async_copy(held.at[chip, n], all_ref.at[n, chip], all_sem.at[n, chip]).wait()

        return carry

    lax.fori_loop(0, len(GIVE[0]), scatter, 0)
    for h in range(2):
        grad_ref[h * half : (h + 1) * half] = outb[mine, h * tokens : (h + 1) * tokens].T

    for c in small:
        c.wait()

    def drain(step, carry):
        cz, cx, chip, n = piece_at(step)
        onward(cz, cx, chip, n, lambda c: c.wait_send())
        return carry

    lax.fori_loop(0, 16, drain, 0)


def weight_grads_kernel(
    hact_ref, pre_ref, x_ref, dy_ref, gate_ref, up_ref, down_ref
):
    bf16 = jnp.bfloat16
    hidden = gate_ref.shape[0]
    both = over_tokens(pre_ref[...], x_ref[0]).astype(bf16)
    gate_ref[...] = both[:hidden]
    up_ref[...] = both[hidden:]
    down_ref[...] = over_tokens(hact_ref[...], dy_ref[0]).astype(bf16)


def on_grid(layer_input, output_grad, gate_weight, up_weight, down_weight):
    chips = 8
    rows, tokens = layer_input.shape
    hidden, features = gate_weight.shape
    width = 2 * rows
    half = rows // 2
    bf16, f32 = jnp.bfloat16, jnp.float32
    anywhere = pl.BlockSpec(memory_space=pl.ANY)
    vmem = pl.BlockSpec(memory_space=pltpu.VMEM)
    DMA = pltpu.SemaphoreType.DMA
    VMEM = pltpu.VMEM
    small = jax.ShapeDtypeStruct((hidden, tokens), bf16)
    grad, hact, pre, gathered = pl.pallas_call(
        grid_kernel,
        out_shape=(
            jax.ShapeDtypeStruct((rows, tokens), bf16),
            small, jax.ShapeDtypeStruct((2, hidden, tokens), bf16),
            jax.ShapeDtypeStruct((2, chips, 2, rows, tokens), bf16),
        ),
        in_specs=[anywhere] * 5,
        out_specs=(vmem, anywhere, anywhere, anywhere),
        scratch_shapes=[
            VMEM((chips, 2, 2, rows, tokens), bf16),
            VMEM((chips, 2 * hidden, width), bf16),
            VMEM((3, hidden, width), bf16),
            VMEM((3, hidden, tokens), f32),
            VMEM((hidden, tokens), bf16),
            VMEM((hidden, tokens), bf16),
            VMEM((hidden, tokens), bf16),
            VMEM((tokens, 2 * hidden), bf16),
            VMEM((chips, 2 * tokens, half), f32),
            VMEM((chips, 2 * tokens, half), bf16),
            VMEM((chips, 2 * tokens, half), bf16),
            VMEM((4, 2 * tokens, half), bf16),
            VMEM((2, chips, 2 * tokens, half), bf16),
            DMA((2,)),
            DMA((3, 2)),
            DMA((4, chips, 2)),
            DMA((chips, 2, 2)),
            DMA((2, chips)),
            DMA((3,)),
            DMA((chips, 2)),
            DMA((chips, 2)),
            DMA((chips, 2)),
            DMA((4, 2)),
            DMA((2, chips, 2)),
        ],
        compiler_params=pltpu.CompilerParams(
            collective_id=0, has_side_effects=True, vmem_limit_bytes=GRID_VMEM
        ),
        name="gather_scatter",
    )(layer_input, output_grad, gate_weight, up_weight, down_weight)
    gathered = gathered.reshape(2, features, tokens)
    block = 1024

    def fixed(shape):
        return pl.BlockSpec(shape, lambda j: (0, 0))

    grads = jax.ShapeDtypeStruct((hidden, features), bf16)
    columns = pl.BlockSpec((hidden, block), lambda j: (0, j))
    gate_grad, up_grad, down_grad = pl.pallas_call(
        weight_grads_kernel,
        grid=(features // block,),
        out_shape=(grads, grads, grads),
        in_specs=[
            fixed((hidden, tokens)),
            fixed((2 * hidden, tokens)),
            pl.BlockSpec((1, block, tokens), lambda j: (0, j, 0)),
            pl.BlockSpec((1, block, tokens), lambda j: (1, j, 0)),
        ],
        out_specs=(columns, columns, columns),
        compiler_params=pltpu.CompilerParams(vmem_limit_bytes=VMEM_LIMIT),
        name="weight_grads",
    )(hact, pre.reshape(2 * hidden, tokens), gathered, gathered)
    return (grad, gate_grad, up_grad, down_grad)


def solution(mesh):
    row = mesh.shape["row"]
    xs = 2 if row <= 16 else 4
    zs = row // (2 * xs)
    return jax.shard_map(
        on_grid if (zs, xs) == (4, 2) else functools.partial(on_device, zs, xs),
        mesh=mesh,
        in_specs=(
            P("row", "groups"),
            P("row", "groups"),
            P(("groups", "row"), None),
            P(("groups", "row"), None),
            P(("groups", "row"), None),
        ),
        out_specs=(
            P("row", "groups"),
            P(("groups", "row"), None),
            P(("groups", "row"), None),
            P(("groups", "row"), None),
        ),
        check_vma=False,
    )
```
